32 devices in a mesh: depth: 16 (over z, y, x), light: 2 (over core).
Axes of the slice: x: 2, y: 2, z: 4, core: 2. Of those that a mesh axis runs over, the one named last changes fastest.
Arguments:
- density: float32 [64, 128, 1024], P('depth', 'light'), may hold values from -6 to 6
- labels: int32 [64, 128, 1024], P('depth', 'light'), may hold values from 0 to 15
- slice_order: int32 [64], P('depth'), may hold values from 0 to 63, as said below
- extinction: float32 [16], replicated, may hold values from 0.0001 to 0.01
- albedo: float32 [3, 16], replicated, may hold values from 0.2 to 1
Outputs:
- image: float32 [4, 131072], P(None, ('light', 'depth'))
The draws below stay inside these ranges and needn't reach their ends.
Inputs may be any that keep to these rules, and one draw needn't show every extreme that they name: Within each aligned block of 4 view positions, slice_order is a permutation of that block's positions.
All inputs are finite; a program needn't handle non-finite values.
Results may differ from the reference program's by a relative error of at most 0.0003.
Values sent between devices are 32-bit elements; how exact they have to be, the bound alone decides.
A program may use at most 64 MiB of HBM per device.

```python
import math
import jax
import jax.numpy as jnp
from jax import lax

DZ = 4
IMAGE_COLUMNS = 1024
NMAT = 16
DEPTH_SLICES = 64
LIGHT_CELLS = 128


def draw_labels(key, part):
    random_keys = jax.random.split(jax.random.fold_in(key, 17), 3)
    ground_label = jax.random.randint(random_keys[0], (DEPTH_SLICES // DZ, 1, IMAGE_COLUMNS), 0, NMAT)
    ground_label = jnp.repeat(ground_label, DZ, axis=0)
    jitter_label = jax.random.randint(random_keys[1], (DEPTH_SLICES, LIGHT_CELLS, IMAGE_COLUMNS), 0, NMAT)
    flare_mask = jax.random.randint(random_keys[2], (DEPTH_SLICES, LIGHT_CELLS, IMAGE_COLUMNS), 0, 8) == 0
    return jnp.where(flare_mask, jitter_label, ground_label).astype(jnp.int32)


def draw_slice_order(key, part):
    bricks = DEPTH_SLICES // DZ
    random_keys = jax.random.split(jax.random.fold_in(key, 29), bricks)
    shuffled = jax.vmap(lambda one_key: jax.random.permutation(one_key, DZ))(random_keys)
    offsets = jnp.arange(bricks, dtype=jnp.int32)[:, None] * DZ
    return (shuffled.astype(jnp.int32) + offsets).reshape(DEPTH_SLICES).astype(jnp.int32)


def steps_of(rng, extent, cuts, least, largest):
    level = 1.0
    for dim, parts in cuts:
        steps = jax.random.uniform(jax.random.fold_in(jax.random.fold_in(rng, 6), dim), (parts,), jnp.float32, least / len(cuts), largest / len(cuts))
        level = level * jnp.repeat(jnp.exp(steps), extent[dim] // parts).reshape((-1,) + (1,) * (len(extent) - 1 - dim))
    return level


def scatter_about(own_key, extent, spread, reach, shards=(), held_as=jnp.bfloat16):
    entries = jax.random.normal(own_key, extent, jnp.float32) * spread
    if len(shards) > 0:
        entries = steps_of(own_key, extent, shards, -0.22, 0.18) * entries
    return jnp.clip(entries, min=-reach, max=reach).astype(held_as)


def setup_inputs(seed: int = 0) -> dict:
    seeds = jax.random.split(jax.random.key(seed), 6)
    return {
        "density": scatter_about(seeds[0], (DEPTH_SLICES, LIGHT_CELLS, IMAGE_COLUMNS), 1.0, 6.0, ((0, 16), (1, 2)), jnp.float32),
        "labels": draw_labels(jax.random.fold_in(seeds[5], 71), 0),
        "slice_order": draw_slice_order(jax.random.fold_in(seeds[5], 71), 0),
        "extinction": jnp.clip(jnp.exp(jax.random.uniform(seeds[3], (NMAT,), jnp.float32, math.log(0.0001), math.log(0.01))), 0.0001, 0.01),
        "albedo": jnp.clip(jax.random.uniform(seeds[4], (3, NMAT), jnp.float32, 0.2, 1.0), 0.2, 1.0),
    }


def smooth_field(padded):
    center = padded[1:-1, 1:-1, 1:-1]
    beside = padded[2:, 1:-1, 1:-1] + padded[:-2, 1:-1, 1:-1]
    beside = beside + padded[1:-1, 2:, 1:-1] + padded[1:-1, :-2, 1:-1]
    beside = beside + padded[1:-1, 1:-1, 2:] + padded[1:-1, 1:-1, :-2]
    return 0.4 * center + 0.1 * beside

def gradient_parts(padded):
    center = padded[1:-1, 1:-1, 1:-1]
    grad_z = 0.5 * (padded[2:, 1:-1, 1:-1] - padded[:-2, 1:-1, 1:-1])
    grad_x = 0.5 * (padded[1:-1, 2:, 1:-1] - padded[1:-1, :-2, 1:-1])
    grad_y = 0.5 * (padded[1:-1, 1:-1, 2:] - padded[1:-1, 1:-1, :-2])
    return (center, grad_z, grad_x, grad_y)

def material_props(materials, extinction, albedo):
    lookup_table = jnp.concatenate([extinction[None, :], albedo], axis=0)
    result = jnp.zeros((4,) + materials.shape, jnp.float32)
    for number in range(NMAT):
        result = jnp.where(materials[None] == number, lookup_table[:, number][:, None, None, None], result)
    return result

def exclusive_sum(values, axis):
    total = jnp.cumsum(values, axis=axis)
    shifted = lax.slice_in_dim(total, 0, values.shape[axis] - 1, axis=axis)
    zero_shape = list(values.shape)
    zero_shape[axis] = 1
    return jnp.concatenate([jnp.zeros(zero_shape, jnp.float32), shifted], axis=axis)

def reference(density, labels, slice_order, extinction, albedo):

    def advance(state_pair, brick_index):
        colour_sum, remaining = state_pair
        view_pos = brick_index * DZ - 2 + jnp.arange(DZ + 4, dtype=jnp.int32)
        inside = (view_pos >= 0) & (view_pos < DEPTH_SLICES)
        stored = jnp.take(slice_order, jnp.clip(view_pos, 0, DEPTH_SLICES - 1).astype(jnp.int32))
        slab_rows = jnp.take(density, stored, axis=0) * inside[:, None, None].astype(jnp.float32)
        padded = jnp.pad(slab_rows, ((0, 0), (2, 2), (2, 2)))
        smoothed = smooth_field(padded)
        x_pos = jnp.arange(LIGHT_CELLS + 2, dtype=jnp.int32)
        y_pos = jnp.arange(IMAGE_COLUMNS + 2, dtype=jnp.int32)
        inside_x = (x_pos >= 1) & (x_pos <= LIGHT_CELLS)
        inside_y = (y_pos >= 1) & (y_pos <= IMAGE_COLUMNS)
        keep_mask = inside[1:-1][:, None, None] & inside_x[None, :, None] & inside_y[None, None, :]
        smoothed = jnp.where(keep_mask, smoothed, jnp.float32(0.0))
        center, grad_z, grad_x, grad_y = gradient_parts(smoothed)
        own_pos = (brick_index * DZ + jnp.arange(DZ, dtype=jnp.int32)).astype(jnp.int32)
        materials = jnp.take(labels, jnp.take(slice_order, own_pos), axis=0)
        material = material_props(materials, extinction, albedo)
        optical = material[0] * jnp.exp(center)
        lighted = jnp.exp(-exclusive_sum(optical, 1))
        opacity = 1.0 - jnp.exp(-optical)
        facing = grad_x / jnp.sqrt(grad_z * grad_z + grad_x * grad_x + grad_y * grad_y + 0.05)
        shading = 0.2 + lighted * (0.5 + 0.5 * facing)
        weight = opacity * shading * jnp.exp(-exclusive_sum(optical, 0))
        colour = lax.optimization_barrier(jnp.sum(material[1:] * weight[None], axis=1))
        colour_sum = colour_sum + remaining[None] * colour
        remaining = remaining * jnp.exp(-lax.optimization_barrier(jnp.sum(optical, axis=0)))
        return ((colour_sum, remaining), brick_index)
    initial = (jnp.zeros((3, LIGHT_CELLS, IMAGE_COLUMNS), jnp.float32), jnp.ones((LIGHT_CELLS, IMAGE_COLUMNS), jnp.float32))
    final_pair, unused = lax.scan(advance, initial, jnp.arange(DEPTH_SLICES // DZ, dtype=jnp.int32))
    colour_sum, remaining = final_pair
    return jnp.concatenate([colour_sum, (1.0 - remaining)[None]], axis=0).reshape(4, LIGHT_CELLS * IMAGE_COLUMNS)
```

```python
import functools

import jax
import jax.numpy as jnp
from jax import lax
from jax.experimental import pallas as pl
from jax.experimental.pallas import tpu as pltpu
from jax.sharding import PartitionSpec as P

SUB, LANE = 8, 128
VMEM_SPEC = pl.BlockSpec(memory_space=pltpu.VMEM)


def reorder_kernel(order_ref, density_ref, labels_ref, viewed_ref, materials_ref):
    rows = density_ref.shape[1]
    viewed_ref[0] = density_ref[0].reshape(rows, SUB, LANE)
    materials_ref[0] = labels_ref[0].reshape(rows, SUB, LANE)


def reorder(density, labels, order):
    slices, rows, columns = density.shape
    source = pl.BlockSpec((1, rows, columns), lambda i, o: (o[i], 0, 0))
    target = pl.BlockSpec((1, rows, SUB, LANE), lambda i, o: (i, 0, 0, 0))
    shape = (slices, rows, SUB, LANE)
    return pl.pallas_call(
        reorder_kernel,
        grid_spec=pltpu.PrefetchScalarGridSpec(
            num_scalar_prefetch=1,
            grid=(slices,),
            in_specs=[source, source],
            out_specs=[target, target],
        ),
        out_shape=[
            jax.ShapeDtypeStruct(shape, density.dtype),
            jax.ShapeDtypeStruct(shape, labels.dtype),
        ],
    )(order, density, labels)


def beside_y(cells, lane, first, last):
    low = pltpu.roll(cells, 1, 1)
    high = pltpu.roll(cells, LANE - 1, 1)
    low = jnp.where(lane == 0, pltpu.roll(low, 1, 0), low)
    high = jnp.where(lane == LANE - 1, pltpu.roll(high, SUB - 1, 0), high)
    return jnp.where(first, 0.0, low), jnp.where(last, 0.0, high)


def lookup(table, index):
    return jnp.take_along_axis(table, index, axis=1, mode="promise_in_bounds")


def shade_kernel(depth_count, light_count, wide, below, above, labels, tables, plain, lit, through, smooth):
    slices, rows = labels.shape[:2]
    depth_at = lax.axis_index("depth")
    light_at = lax.axis_index("light")
    lane = lax.broadcasted_iota(jnp.int32, (SUB, LANE), 1)
    sub = lax.broadcasted_iota(jnp.int32, (SUB, LANE), 0)
    first = (lane == 0) & (sub == 0)
    last = (lane == LANE - 1) & (sub == SUB - 1)
    has_below = (depth_at > 0).astype(jnp.float32)
    has_above = (depth_at < depth_count - 1).astype(jnp.float32)
    has_before = (light_at > 0).astype(jnp.float32)
    has_after = (light_at < light_count - 1).astype(jnp.float32)

    def cell(z, row):
        if z < 0:
            return below[z + 2, row]
        if z >= slices:
            return above[z - slices, row]
        return wide[z, row]

    def smooth_row(i, carry):
        column = [cell(z, i + 1) for z in range(-2, slices + 2)]
        for z in range(-1, slices + 1):
            center = column[z + 2]
            low, high = beside_y(center, lane, first, last)
            total = (column[z + 1] + column[z + 3]) + (cell(z, i) + cell(z, i + 2)) + (low + high)
            value = 0.4 * center + 0.1 * total
            if z < 0:
                value = value * has_below
            if z >= slices:
                value = value * has_above
            smooth[z + 1, i] = value
        return carry

    lax.fori_loop(0, rows + 2, smooth_row, 0)
    for z in range(slices):
        smooth[z + 1, 0] = smooth[z + 1, 0] * has_before
        smooth[z + 1, rows + 1] = smooth[z + 1, rows + 1] * has_after

    def shade_row(r, lights):
        lights = list(lights)
        remaining = jnp.ones((SUB, LANE), jnp.float32)
        flat = [jnp.zeros((SUB, LANE), jnp.float32) for _ in range(3)]
        for z in range(slices):
            center = smooth[z + 1, r + 1]
            low, high = beside_y(center, lane, first, last)
            grad_z = smooth[z + 2, r + 1] - smooth[z, r + 1]
            grad_x = smooth[z + 1, r + 2] - smooth[z + 1, r]
            grad_y = high - low
            facing = grad_x * lax.rsqrt(grad_z * grad_z + grad_x * grad_x + grad_y * grad_y + 0.2)
            index = labels[z, r]
            optical = lookup(tables[0], index) * jnp.exp(center)
            passed = jnp.exp(-optical)
            weight = (1.0 - passed) * remaining
            glow = weight * lights[z] * (0.5 + 0.5 * facing)
            faint = 0.2 * weight
            for c in range(3):
                albedo = lookup(tables[c + 1], index)
                flat[c] = flat[c] + albedo * faint
                lit[z * 3 + c, r] = albedo * glow
            remaining = remaining * passed
            lights[z] = lights[z] * passed
        for c in range(3):
            plain[c, r] = flat[c]
        plain[3, r] = 1.0 - remaining
        return tuple(lights)

    ones = tuple(jnp.ones((SUB, LANE), jnp.float32) for _ in range(slices))
    lights = lax.fori_loop(0, rows, shade_row, ones)
    for z in range(slices):
        through[z] = lights[z]


def shade(wide, below, above, labels, tables, depth_count, light_count):
    slices, rows = labels.shape[:2]
    f32 = jnp.float32
    return pl.pallas_call(
        functools.partial(shade_kernel, depth_count, light_count),
        in_specs=[VMEM_SPEC] * 5,
        out_specs=[VMEM_SPEC] * 3,
        out_shape=[
            jax.ShapeDtypeStruct((4, rows, SUB, LANE), f32),
            jax.ShapeDtypeStruct((slices * 3, rows, SUB, LANE), f32),
            jax.ShapeDtypeStruct((slices, SUB, LANE), f32),
        ],
        scratch_shapes=[pltpu.VMEM((slices + 2, rows + 2, SUB, LANE), f32)],
        compiler_params=pltpu.CompilerParams(vmem_limit_bytes=48 * 1024 * 1024),
    )(wide, below, above, labels, tables)


def both_ways(low_part, high_part, axis, count):
    from_low = lax.ppermute(high_part, axis, [(i, i + 1) for i in range(count - 1)])
    from_high = lax.ppermute(low_part, axis, [(i + 1, i) for i in range(count - 1)])
    return from_low, from_high


def partner(block, axis, stride):
    count = lax.axis_size(axis)
    route = []
    for low in range(count):
        high = low | 1 << stride
        if high != low and high < count:
            route += [(low, high), (high, low)]
    return lax.ppermute(block, axis, route)


def over_blend(front_part, back_part):
    return front_part + (1.0 - front_part[3:4]) * back_part


def shards(density, labels, slice_order, extinction, albedo):
    depth_count = lax.axis_size("depth")
    light_count = lax.axis_size("light")
    depth_at = lax.axis_index("depth")
    light_at = lax.axis_index("light")
    slices, rows, columns = density.shape
    viewed, materials = reorder(density, labels, slice_order % slices)
    before, after = both_ways(viewed[:, :2], viewed[:, -2:], "light", light_count)
    wide = jnp.concatenate([before, viewed, after], axis=1)
    below, above = both_ways(wide[:2], wide[-2:], "depth", depth_count)
    tables = jnp.concatenate([extinction[None, :], albedo], axis=0)
    tables = jnp.pad(tables, ((0, 0), (0, LANE - tables.shape[1])))
    tables = jnp.broadcast_to(tables[:, None, :], (4, SUB, LANE))
    plain, lit, through = shade(wide, below, above, materials, tables, depth_count, light_count)
    gathered = lax.all_gather(through, "light")
    incoming = jnp.ones_like(through)
    for k in range(light_count - 1):
        incoming = jnp.where(k < light_at, incoming * gathered[k], incoming)
    lit = lit.reshape(slices, 3, rows, SUB, LANE) * incoming[:, None, None]
    colour = plain[:3] + jnp.sum(lit, axis=0)
    current = jnp.concatenate([colour, plain[3:]], axis=0)
    current = current.reshape(4, depth_count, rows // depth_count if rows >= depth_count else 1, SUB, -1)
    for bit_number in range(depth_count.bit_length() - 1):
        blocks = current.shape[1]
        halves = current.reshape((4, blocks // 2, 2) + current.shape[2:])
        upper_bit = depth_at >> bit_number & 1
        kept_half = lax.dynamic_index_in_dim(halves, upper_bit, 2, False)
        given_half = lax.dynamic_index_in_dim(halves, 1 - upper_bit, 2, False)
        taken_half = partner(given_half, "depth", bit_number)
        in_front = jnp.where(upper_bit == 0, kept_half, taken_half)
        behind = jnp.where(upper_bit == 0, taken_half, kept_half)
        current = over_blend(in_front, behind)
    return current.reshape(4, -1)


def solution(mesh):
    return jax.shard_map(
        shards,
        mesh=mesh,
        in_specs=(P("depth", "light", None), P("depth", "light", None), P("depth"), P(), P()),
        out_specs=P(None, ("light", "depth")),
        check_vma=False,
    )
```

```python
import functools

import jax
import jax.numpy as jnp
from jax import lax
from jax.experimental import pallas as pl
from jax.experimental.pallas import tpu as pltpu
from jax.sharding import PartitionSpec as P

SUB, LANE = 8, 128
MESH = pl.DeviceIdType.MESH
VMEM_SPEC = pl.BlockSpec(memory_space=pltpu.VMEM)


def reorder_kernel(order_ref, density_ref, labels_ref, viewed_ref, materials_ref):
    rows = density_ref.shape[1]
    viewed_ref[0] = density_ref[0].reshape(rows, SUB, LANE)
    materials_ref[0] = labels_ref[0].reshape(rows, SUB, LANE)


def reorder(density, labels, order):
    slices, rows, columns = density.shape
    source = pl.BlockSpec((1, rows, columns), lambda i, o: (o[i], 0, 0))
    target = pl.BlockSpec((1, rows, SUB, LANE), lambda i, o: (i, 0, 0, 0))
    shape = (slices, rows, SUB, LANE)
    return pl.pallas_call(
        reorder_kernel,
        grid_spec=pltpu.PrefetchScalarGridSpec(
            num_scalar_prefetch=1,
            grid=(slices,),
            in_specs=[source, source],
            out_specs=[target, target],
        ),
        out_shape=[
            jax.ShapeDtypeStruct(shape, density.dtype),
            jax.ShapeDtypeStruct(shape, labels.dtype),
        ],
    )(order, density, labels)


def beside_y(cells, lane, first, last):
    low = pltpu.roll(cells, 1, 1)
    high = pltpu.roll(cells, LANE - 1, 1)
    low = jnp.where(lane == 0, pltpu.roll(low, 1, 0), low)
    high = jnp.where(lane == LANE - 1, pltpu.roll(high, SUB - 1, 0), high)
    return jnp.where(first, 0.0, low), jnp.where(last, 0.0, high)


def lookup(table, index):
    return jnp.take_along_axis(table, index, axis=1, mode="promise_in_bounds")


def shade_kernel(depth_count, light_count, volume, labels, tables, plain, lit, through, smooth):
    slices, rows = labels.shape[:2]
    depth_at = lax.axis_index("depth")
    light_at = lax.axis_index("light")
    pair_at = depth_at // 2
    stripe_at = light_at * 2 + depth_at % 2
    lane = lax.broadcasted_iota(jnp.int32, (SUB, LANE), 1)
    sub = lax.broadcasted_iota(jnp.int32, (SUB, LANE), 0)
    first = (lane == 0) & (sub == 0)
    last = (lane == LANE - 1) & (sub == SUB - 1)
    has_below = (pair_at > 0).astype(jnp.float32)
    has_above = (pair_at < depth_count // 2 - 1).astype(jnp.float32)
    has_before = (stripe_at > 0).astype(jnp.float32)
    has_after = (stripe_at < 2 * light_count - 1).astype(jnp.float32)

    def cell(z, row):
        return volume[z + 2, row]

    def smooth_row(i, carry):
        column = [cell(z, i + 1) for z in range(-2, slices + 2)]
        for z in range(-1, slices + 1):
            center = column[z + 2]
            low, high = beside_y(center, lane, first, last)
            total = (column[z + 1] + column[z + 3]) + (cell(z, i) + cell(z, i + 2)) + (low + high)
            value = 0.4 * center + 0.1 * total
            if z < 0:
                value = value * has_below
            if z >= slices:
                value = value * has_above
            smooth[z + 1, i] = value
        return carry

    lax.fori_loop(0, rows + 2, smooth_row, 0)
    for z in range(slices):
        smooth[z + 1, 0] = smooth[z + 1, 0] * has_before
        smooth[z + 1, rows + 1] = smooth[z + 1, rows + 1] * has_after

    def shade_row(r, lights):
        lights = list(lights)
        remaining = jnp.ones((SUB, LANE), jnp.float32)
        flat = [jnp.zeros((SUB, LANE), jnp.float32) for _ in range(3)]
        for z in range(slices):
            center = smooth[z + 1, r + 1]
            low, high = beside_y(center, lane, first, last)
            grad_z = smooth[z + 2, r + 1] - smooth[z, r + 1]
            grad_x = smooth[z + 1, r + 2] - smooth[z + 1, r]
            grad_y = high - low
            facing = grad_x * lax.rsqrt(grad_z * grad_z + grad_x * grad_x + grad_y * grad_y + 0.2)
            index = labels[z, r]
            optical = lookup(tables[0], index) * jnp.exp(center)
            passed = jnp.exp(-optical)
            weight = (1.0 - passed) * remaining
            glow = weight * lights[z] * (0.5 + 0.5 * facing)
            faint = 0.2 * weight
            for c in range(3):
                albedo = lookup(tables[c + 1], index)
                flat[c] = flat[c] + albedo * faint
                lit[z * 3 + c, r] = albedo * glow
            remaining = remaining * passed
            lights[z] = lights[z] * passed
        for c in range(3):
            plain[c, r] = flat[c]
        plain[3, r] = 1.0 - remaining
        return tuple(lights)

    ones = tuple(jnp.ones((SUB, LANE), jnp.float32) for _ in range(slices))
    lights = lax.fori_loop(0, rows, shade_row, ones)
    for z in range(slices):
        through[z] = lights[z]


def shade(volume, labels, tables, depth_count, light_count):
    slices, rows = labels.shape[:2]
    f32 = jnp.float32
    return pl.pallas_call(
        functools.partial(shade_kernel, depth_count, light_count),
        in_specs=[VMEM_SPEC] * 3,
        out_specs=[VMEM_SPEC] * 3,
        out_shape=[
            jax.ShapeDtypeStruct((4, rows, SUB, LANE), f32),
            jax.ShapeDtypeStruct((slices * 3, rows, SUB, LANE), f32),
            jax.ShapeDtypeStruct((slices, SUB, LANE), f32),
        ],
        scratch_shapes=[pltpu.VMEM((slices + 2, rows + 2, SUB, LANE), f32)],
        compiler_params=pltpu.CompilerParams(vmem_limit_bytes=40 * 1024 * 1024),
    )(volume, labels, tables)


def greet(wanted):
    barrier = pltpu.get_barrier_semaphore()
    count = 0
    for exists, depth, light in wanted:

        @pl.when(exists)
        def _():
            pl.semaphore_signal(barrier, inc=1, device_id=(depth, light), device_id_type=MESH)

        count = count + jnp.where(exists, 1, 0)
    pl.semaphore_wait(barrier, count)


def trade_kernel(depth_count, light_count, viewed, materials, volume, labels, local_sem, send_sem, recv_sem):
    slices, rows = viewed.shape[:2]
    half = rows // 2
    depth_at = lax.axis_index("depth")
    light_at = lax.axis_index("light")
    side = depth_at % 2
    pair = depth_at // 2
    even = pair * 2
    other = even + 1 - side
    has_below = pair > 0
    has_above = pair < depth_count // 2 - 1
    has_before = light_at > 0
    has_after = light_at < light_count - 1
    own = 2 + slices * side
    wanted = [(depth_at >= 0, other, light_at)]
    for exists, light in ((has_before, light_at - 1), (has_after, light_at + 1)):
        wanted += [(exists, even, light), (exists, even + 1, light)]
    wanted += [(has_below, depth_at - 2, light_at), (has_above, depth_at + 2, light_at)]

    def piece(to_side):
        return viewed.at[:, pl.ds((half - 2) * to_side, half + 2)]

    def spot(from_side, to_side):
        return volume.at[pl.ds(2 + slices * from_side, slices), pl.ds(2 - 2 * to_side, half + 2)]

    keep = pltpu.make_async_copy(piece(side), spot(side, side), local_sem.at[0])
    keep_labels = pltpu.make_async_copy(
        materials.at[:, pl.ds(half * side, half)], labels.at[pl.ds(slices * side, slices)], local_sem.at[1]
    )
    keep.start()
    keep_labels.start()
    zeros2 = jnp.zeros((2, half + 4, SUB, LANE), jnp.float32)
    zerosr = jnp.zeros((volume.shape[0] - 4, 2, SUB, LANE), jnp.float32)

    @pl.when(jnp.logical_not(has_below))
    def _():
        volume[0:2] = zeros2

    @pl.when(jnp.logical_not(has_above))
    def _():
        volume[2 * slices + 2 :] = zeros2

    @pl.when(jnp.logical_not(has_before) & (side == 0))
    def _():
        volume[2 : 2 * slices + 2, 0:2] = zerosr

    @pl.when(jnp.logical_not(has_after) & (side == 1))
    def _():
        volume[2 : 2 * slices + 2, half + 2 : half + 4] = zerosr

    greet(wanted)

    def remote(source, target, slot, depth, light):
        return pltpu.make_async_remote_copy(
            src_ref=source,
            dst_ref=target,
            send_sem=send_sem.at[slot],
            recv_sem=recv_sem.at[slot],
            device_id=(depth, light),
            device_id_type=MESH,
        )

    swaps = []
    for part in range(2):
        two = slices // 2
        swaps.append(
            remote(
                viewed.at[pl.ds(part * two, two), pl.ds((half - 2) * (1 - side), half + 2)],
                volume.at[pl.ds(own + part * two, two), pl.ds(2 * side, half + 2)],
                part,
                other,
                light_at,
            )
        )
    swaps.append(
        remote(
            materials.at[:, pl.ds(half * (1 - side), half)], labels.at[pl.ds(slices * side, slices)], 2, other, light_at
        )
    )

    def to_after(sender):
        return volume.at[pl.ds(2 + slices * sender, slices), 0:2]

    def to_before(sender):
        return volume.at[pl.ds(2 + slices * sender, slices), half + 2 : half + 4]

    def rim(source, target, slot, depth, light):
        return pltpu.make_async_remote_copy(
            src_ref=source,
            dst_ref=target,
            send_sem=send_sem.at[slot],
            recv_sem=recv_sem.at[3 + side],
            device_id=(depth, light),
            device_id_type=MESH,
        )

    after_rim = rim(viewed.at[:, rows - 2 : rows], to_after(side), 3, even, light_at + 1)
    before_rim = rim(viewed.at[:, 0:2], to_before(side), 4, even + 1, light_at - 1)

    @pl.when(has_after)
    def _():
        after_rim.start()

    @pl.when(has_before)
    def _():
        before_rim.start()

    @pl.when(side == 0)
    def _():
        swaps[0].start()
        swaps[1].start()

    @pl.when(side == 1)
    def _():
        swaps[1].start()
        swaps[0].start()

    swaps[2].start()

    def rim_wait(sender):
        return pltpu.make_async_remote_copy(
            src_ref=to_after(sender),
            dst_ref=to_after(sender),
            send_sem=send_sem.at[3],
            recv_sem=recv_sem.at[3 + sender],
            device_id=(other, light_at),
            device_id_type=MESH,
        )

    @pl.when((has_before & (side == 0)) | (has_after & (side == 1)))
    def _():
        rim_wait(0).wait_recv()
        rim_wait(1).wait_recv()

    keep.wait()
    below = remote(volume.at[2:4], volume.at[2 * slices + 2 : 2 * slices + 4], 5, depth_at - 2, light_at)
    above = remote(volume.at[2 * slices : 2 * slices + 2], volume.at[0:2], 6, depth_at + 2, light_at)

    @pl.when((side == 0) & has_below)
    def _():
        below.start()

    @pl.when((side == 1) & has_above)
    def _():
        above.start()

    @pl.when(side == 0)
    def _():
        swaps[1].wait_recv()

    @pl.when(side == 1)
    def _():
        swaps[0].wait_recv()

    @pl.when((side == 1) & has_below)
    def _():
        below.start()

    @pl.when((side == 0) & has_above)
    def _():
        above.start()

    @pl.when(side == 0)
    def _():
        swaps[0].wait_recv()

    @pl.when(side == 1)
    def _():
        swaps[1].wait_recv()

    swaps[2].wait_recv()
    keep_labels.wait()

    @pl.when(has_above)
    def _():
        below.wait_recv()

    @pl.when(has_below)
    def _():
        above.wait_recv()

    for one in swaps:
        one.wait_send()

    @pl.when(has_below)
    def _():
        below.wait_send()

    @pl.when(has_above)
    def _():
        above.wait_send()

    @pl.when(has_after)
    def _():
        after_rim.wait_send()

    @pl.when(has_before)
    def _():
        before_rim.wait_send()


def trade(viewed, materials, depth_count, light_count):
    slices, rows = viewed.shape[:2]
    half = rows // 2
    return pl.pallas_call(
        functools.partial(trade_kernel, depth_count, light_count),
        in_specs=[VMEM_SPEC] * 2,
        out_specs=[VMEM_SPEC] * 2,
        out_shape=[
            jax.ShapeDtypeStruct((2 * slices + 4, half + 4, SUB, LANE), jnp.float32),
            jax.ShapeDtypeStruct((2 * slices, half, SUB, LANE), jnp.int32),
        ],
        scratch_shapes=[
            pltpu.SemaphoreType.DMA((2,)),
            pltpu.SemaphoreType.DMA((7,)),
            pltpu.SemaphoreType.DMA((7,)),
        ],
        compiler_params=pltpu.CompilerParams(
            collective_id=0, has_side_effects=True, vmem_limit_bytes=20 * 1024 * 1024
        ),
    )(viewed, materials)


def over_blend(front, back):
    through = 1.0 - front[3:4]
    return front + through * back


def merge_kernel(depth_count, light_count, plain, lit, through, image, blocks, *rest):
    stages = depth_count.bit_length() - 3
    taken = rest[:stages]
    ends, shadow, send_sem, recv_sem, end_send, end_recv, shadow_send, shadow_recv = rest[stages:]
    slices = through.shape[0]
    block_rows = blocks.shape[2]
    block_count = depth_count // 2
    stripes = 2 * light_count
    depth_at = lax.axis_index("depth")
    light_at = lax.axis_index("light")
    side = depth_at % 2
    pair = depth_at // 2
    stripe = light_at * 2 + side
    top = pair // (block_count // 2)
    low_bits = pair % (block_count // 2)

    def flipped(b):
        bit = (pair // (1 << b)) % 2
        return bit, (pair + (1 - 2 * bit) * (1 << b)) * 2 + side

    end_base = 2 * (side * (block_count // 2) + low_bits)
    source0 = 2 * low_bits + top
    source1 = 2 * (low_bits + block_count // 2) + top
    wanted = [(k != stripe, pair * 2 + k % 2, k // 2) for k in range(stripes)]
    wanted += [(depth_at >= 0, flipped(b)[1], light_at) for b in range(stages)]
    for x in range(2):
        wanted.append((end_base + x != depth_at, end_base + x, light_at))
    ends_from = [(source0 != depth_at, source0), (source1 != depth_at, source1)]
    wanted += [(exists, depth, light_at) for exists, depth in ends_from]
    greet(wanted)

    def shadow_copy(k, slot):
        return pltpu.make_async_remote_copy(
            src_ref=through,
            dst_ref=shadow.at[slot],
            send_sem=shadow_send.at[k],
            recv_sem=shadow_recv.at[slot],
            device_id=(pair * 2 + k % 2, k // 2),
            device_id_type=MESH,
        )

    for k in range(1, stripes):

        @pl.when(k > stripe)
        def _():
            shadow_copy(k, stripe).start()

    for z in range(slices):
        shadow[stripes, z] = jnp.ones((SUB, LANE), jnp.float32)
    for k in range(stripes - 1):

        @pl.when(k < stripe)
        def _():
            shadow_copy(k, k).wait_recv()
            for z in range(slices):
                shadow[stripes, z] = shadow[stripes, z] * shadow[k, z]

    lights = [shadow[stripes, z] for z in range(slices)]

    def finish(block):
        def one_row(i, carry):
            row = block * block_rows + i
            for c in range(3):
                value = plain[c, row]
                for z in range(slices):
                    value = value + lights[z] * lit[z * 3 + c, row]
                blocks[block, c, i] = value
            blocks[block, 3, i] = plain[3, row]
            return carry

        lax.fori_loop(0, block_rows, one_row, 0)

    def index_of(b, n, bit):
        x, upper = n % 2, n // 2
        return x + 2 * ((pair % (1 << b)) + (bit + 2 * upper) * (1 << b))

    def swap(b, n):
        bit, depth = flipped(b)
        slot = block_count - (block_count >> b) + n
        return pltpu.make_async_remote_copy(
            src_ref=blocks.at[index_of(b, n, 1 - bit)],
            dst_ref=taken[b].at[n],
            send_sem=send_sem.at[slot],
            recv_sem=recv_sem.at[slot],
            device_id=(depth, light_at),
            device_id_type=MESH,
        )

    count0 = block_count // 2
    bit0 = pair % 2
    for n in range(count0):
        finish(index_of(0, n, 1 - bit0))
        swap(0, n).start()
    for n in range(count0):
        finish(index_of(0, n, bit0))

    def blend_into(front_ref, back_ref, target_ref):
        for i in range(block_rows):
            clear = 1.0 - front_ref[3, i]
            for c in range(4):
                target_ref[c, i] = front_ref[c, i] + clear * back_ref[c, i]

    def blend(b, n):
        bit, depth = flipped(b)
        swap(b, n).wait_recv()
        mine = blocks.at[index_of(b, n, bit)]

        @pl.when(bit == 0)
        def _():
            blend_into(mine, taken[b].at[n], mine)

        @pl.when(bit == 1)
        def _():
            blend_into(taken[b].at[n], mine, mine)

    def end_copy(x, slot):
        return pltpu.make_async_remote_copy(
            src_ref=blocks.at[x + 2 * low_bits],
            dst_ref=ends.at[slot],
            send_sem=end_send.at[x],
            recv_sem=end_recv.at[slot],
            device_id=(end_base + x, light_at),
            device_id_type=MESH,
        )

    for b in range(stages):
        count = block_count >> (b + 1)
        bit, depth = flipped(b)
        if b + 1 < stages:
            for n in range(count):
                blend(b, n)
            for n in range(count // 2):
                swap(b + 1, n).start()
        else:
            for n in range(count):
                blend(b, n)
    for x in range(2):

        @pl.when(end_base + x != depth_at)
        def _():
            end_copy(x, top).start()

    stay = source0 == depth_at
    stay_late = source1 == depth_at
    mine = blocks.at[side + 2 * low_bits]

    @pl.when(jnp.logical_not(stay))
    def _():
        end_copy(0, 0).wait_recv()

    @pl.when(jnp.logical_not(stay_late))
    def _():
        end_copy(0, 1).wait_recv()

    @pl.when(stay)
    def _():
        blend_into(mine, ends.at[1], image)

    @pl.when(stay_late)
    def _():
        blend_into(ends.at[0], mine, image)

    @pl.when(jnp.logical_not(stay | stay_late))
    def _():
        blend_into(ends.at[0], ends.at[1], image)

    for b in range(stages):
        for n in range(block_count >> (b + 1)):
            swap(b, n).wait_send()
    for x in range(2):

        @pl.when(end_base + x != depth_at)
        def _():
            end_copy(x, top).wait_send()

    for k in range(1, stripes):

        @pl.when(k > stripe)
        def _():
            shadow_copy(k, stripe).wait_send()


def merge(plain, lit, through, depth_count, light_count):
    rows, slices = plain.shape[1], through.shape[0]
    f32 = jnp.float32
    block_count = depth_count // 2
    block = (4, rows // block_count, SUB, LANE)
    stages = depth_count.bit_length() - 3
    stripes = 2 * light_count
    dma = pltpu.SemaphoreType.DMA
    scratch = [pltpu.VMEM((block_count,) + block, f32)]
    scratch += [pltpu.VMEM((block_count >> (b + 1),) + block, f32) for b in range(stages)]
    scratch += [pltpu.VMEM((2,) + block, f32), pltpu.VMEM((stripes + 1, slices, SUB, LANE), f32)]
    scratch += [dma((block_count,)), dma((block_count,)), dma((2,)), dma((2,)), dma((stripes,)), dma((stripes,))]
    return pl.pallas_call(
        functools.partial(merge_kernel, depth_count, light_count),
        in_specs=[VMEM_SPEC] * 3,
        out_specs=VMEM_SPEC,
        out_shape=jax.ShapeDtypeStruct(block, f32),
        scratch_shapes=scratch,
        compiler_params=pltpu.CompilerParams(
            collective_id=1, has_side_effects=True, vmem_limit_bytes=40 * 1024 * 1024
        ),
    )(plain, lit, through)


def shards(density, labels, slice_order, extinction, albedo):
    depth_count = lax.axis_size("depth")
    light_count = lax.axis_size("light")
    slices, rows, columns = density.shape
    viewed, materials = reorder(density, labels, slice_order % slices)
    volume, stripe_labels = trade(viewed, materials, depth_count, light_count)
    tables = jnp.concatenate([extinction[None, :], albedo], axis=0)
    tables = jnp.pad(tables, ((0, 0), (0, LANE - tables.shape[1])))
    tables = jnp.broadcast_to(tables[:, None, :], (4, SUB, LANE))
    plain, lit, through = shade(volume, stripe_labels, tables, depth_count, light_count)
    return merge(plain, lit, through, depth_count, light_count).reshape(4, -1)


def solution(mesh):
    return jax.shard_map(
        shards,
        mesh=mesh,
        in_specs=(P("depth", "light", None), P("depth", "light", None), P("depth"), P(), P()),
        out_specs=P(None, ("light", "depth")),
        check_vma=False,
    )
```

```python
import functools

import jax
import jax.numpy as jnp
from jax import lax
from jax.experimental import pallas as pl
from jax.experimental.pallas import tpu as pltpu
from jax.sharding import PartitionSpec as P

SUB, LANE = 8, 128
MESH = pl.DeviceIdType.MESH
VMEM_SPEC = pl.BlockSpec(memory_space=pltpu.VMEM)


def reorder_kernel(order, density, labels, viewed, materials, held, held_labels, sems):
    slices, rows = density.shape[:2]
    copies = []
    for source, target, base in ((density, held, 0), (labels, held_labels, slices)):
        for z in range(slices):
            at = lax.rem(order[z], slices)
            copies.append(pltpu.make_async_copy(source.at[at], target.at[z], sems.at[base + z]))
    for one in copies:
        one.start()
    for z in range(slices):
        copies[z].wait()
        viewed[z] = held[z].reshape(rows, SUB, LANE)
    for z in range(slices):
        copies[slices + z].wait()
        materials[z] = held_labels[z].reshape(rows, SUB, LANE)


def reorder(density, labels, order):
    slices, rows, columns = density.shape
    shape = (slices, rows, SUB, LANE)
    far = pl.BlockSpec(memory_space=pltpu.HBM)
    return pl.pallas_call(
        reorder_kernel,
        in_specs=[pl.BlockSpec(memory_space=pltpu.SMEM), far, far],
        out_specs=[VMEM_SPEC] * 2,
        out_shape=[
            jax.ShapeDtypeStruct(shape, density.dtype),
            jax.ShapeDtypeStruct(shape, labels.dtype),
        ],
        scratch_shapes=[
            pltpu.VMEM(density.shape, density.dtype),
            pltpu.VMEM(labels.shape, labels.dtype),
            pltpu.SemaphoreType.DMA((2 * slices,)),
        ],
        compiler_params=pltpu.CompilerParams(vmem_limit_bytes=12 * 1024 * 1024),
    )(order, density, labels)


def beside_y(cells, lane, first, last):
    low = pltpu.roll(cells, 1, 1)
    high = pltpu.roll(cells, LANE - 1, 1)
    low = jnp.where(lane == 0, pltpu.roll(low, 1, 0), low)
    high = jnp.where(lane == LANE - 1, pltpu.roll(high, SUB - 1, 0), high)
    return jnp.where(first, 0.0, low), jnp.where(last, 0.0, high)


def lookup(table, index):
    return jnp.take_along_axis(table, index, axis=1, mode="promise_in_bounds")


def shade_kernel(depth_count, light_count, volume, labels, extinction, albedo, plain, lit, through, smooth):
    slices, rows = labels.shape[:2]
    depth_at = lax.axis_index("depth")
    light_at = lax.axis_index("light")
    pair_at = depth_at // 2
    stripe_at = light_at * 2 + depth_at % 2
    lane = lax.broadcasted_iota(jnp.int32, (SUB, LANE), 1)
    sub = lax.broadcasted_iota(jnp.int32, (SUB, LANE), 0)
    first = (lane == 0) & (sub == 0)
    last = (lane == LANE - 1) & (sub == SUB - 1)
    tables = [jnp.zeros((SUB, LANE), jnp.float32) for _ in range(4)]
    for k in range(extinction.shape[0]):
        tables[0] = jnp.where(lane == k, extinction[k], tables[0])
        for c in range(3):
            tables[c + 1] = jnp.where(lane == k, albedo[c, k], tables[c + 1])
    has_below = (pair_at > 0).astype(jnp.float32)
    has_above = (pair_at < depth_count // 2 - 1).astype(jnp.float32)
    has_before = (stripe_at > 0).astype(jnp.float32)
    has_after = (stripe_at < 2 * light_count - 1).astype(jnp.float32)

    def cell(z, row):
        return volume[z + 2, row]

    def smooth_row(i, carry):
        column = [cell(z, i + 1) for z in range(-2, slices + 2)]
        for z in range(-1, slices + 1):
            center = column[z + 2]
            low, high = beside_y(center, lane, first, last)
            total = (column[z + 1] + column[z + 3]) + (cell(z, i) + cell(z, i + 2)) + (low + high)
            value = 0.4 * center + 0.1 * total
            if z < 0:
                value = value * has_below
            if z >= slices:
                value = value * has_above
            smooth[z + 1, i] = value
        return carry

    lax.fori_loop(0, rows + 2, smooth_row, 0)
    for z in range(slices):
        smooth[z + 1, 0] = smooth[z + 1, 0] * has_before
        smooth[z + 1, rows + 1] = smooth[z + 1, rows + 1] * has_after

    def shade_row(r, lights):
        lights = list(lights)
        remaining = jnp.ones((SUB, LANE), jnp.float32)
        flat = [jnp.zeros((SUB, LANE), jnp.float32) for _ in range(3)]
        for z in range(slices):
            center = smooth[z + 1, r + 1]
            low, high = beside_y(center, lane, first, last)
            grad_z = smooth[z + 2, r + 1] - smooth[z, r + 1]
            grad_x = smooth[z + 1, r + 2] - smooth[z + 1, r]
            grad_y = high - low
            facing = grad_x * lax.rsqrt(grad_z * grad_z + grad_x * grad_x + grad_y * grad_y + 0.2)
            index = labels[z, r]
            optical = lookup(tables[0], index) * jnp.exp(center)
            passed = jnp.exp(-optical)
            weight = (1.0 - passed) * remaining
            glow = weight * lights[z] * (0.5 + 0.5 * facing)
            faint = 0.2 * weight
            for c in range(3):
                tint = lookup(tables[c + 1], index)
                flat[c] = flat[c] + tint * faint
                lit[z * 3 + c, r] = tint * glow
            remaining = remaining * passed
            lights[z] = lights[z] * passed
        for c in range(3):
            plain[c, r] = flat[c]
        plain[3, r] = 1.0 - remaining
        return tuple(lights)

    ones = tuple(jnp.ones((SUB, LANE), jnp.float32) for _ in range(slices))
    lights = lax.fori_loop(0, rows, shade_row, ones)
    for z in range(slices):
        through[z] = lights[z]


def shade(volume, labels, extinction, albedo, depth_count, light_count):
    slices, rows = labels.shape[:2]
    f32 = jnp.float32
    return pl.pallas_call(
        functools.partial(shade_kernel, depth_count, light_count),
        in_specs=[VMEM_SPEC] * 2 + [pl.BlockSpec(memory_space=pltpu.SMEM)] * 2,
        out_specs=[VMEM_SPEC] * 3,
        out_shape=[
            jax.ShapeDtypeStruct((4, rows, SUB, LANE), f32),
            jax.ShapeDtypeStruct((slices * 3, rows, SUB, LANE), f32),
            jax.ShapeDtypeStruct((slices, SUB, LANE), f32),
        ],
        scratch_shapes=[pltpu.VMEM((slices + 2, rows + 2, SUB, LANE), f32)],
        compiler_params=pltpu.CompilerParams(vmem_limit_bytes=40 * 1024 * 1024),
    )(volume, labels, extinction, albedo)


def greet(wanted):
    barrier = pltpu.get_barrier_semaphore()
    count = 0
    for exists, depth, light in wanted:

        @pl.when(exists)
        def _():
            pl.semaphore_signal(barrier, inc=1, device_id=(depth, light), device_id_type=MESH)

        count = count + jnp.where(exists, 1, 0)
    pl.semaphore_wait(barrier, count)


def trade_kernel(depth_count, light_count, viewed, materials, volume, labels, local_sem, send_sem, recv_sem):
    slices, rows = viewed.shape[:2]
    half = rows // 2
    depth_at = lax.axis_index("depth")
    light_at = lax.axis_index("light")
    side = depth_at % 2
    pair = depth_at // 2
    even = pair * 2
    other = even + 1 - side
    has_below = pair > 0
    has_above = pair < depth_count // 2 - 1
    has_before = light_at > 0
    has_after = light_at < light_count - 1
    own = 2 + slices * side
    wanted = [(depth_at >= 0, other, light_at)]
    for exists, light in ((has_before, light_at - 1), (has_after, light_at + 1)):
        wanted += [(exists, even, light), (exists, even + 1, light)]
    wanted += [(has_below, depth_at - 2, light_at), (has_above, depth_at + 2, light_at)]

    def piece(to_side):
        return viewed.at[:, pl.ds((half - 2) * to_side, half + 2)]

    def spot(from_side, to_side):
        return volume.at[pl.ds(2 + slices * from_side, slices), pl.ds(2 - 2 * to_side, half + 2)]

    keep = pltpu.make_async_copy(piece(side), spot(side, side), local_sem.at[0])
    keep_labels = pltpu.make_async_copy(
        materials.at[:, pl.ds(half * side, half)], labels.at[pl.ds(slices * side, slices)], local_sem.at[1]
    )
    keep.start()
    keep_labels.start()
    zeros2 = jnp.zeros((2, half + 4, SUB, LANE), jnp.float32)
    zerosr = jnp.zeros((volume.shape[0] - 4, 2, SUB, LANE), jnp.float32)

    @pl.when(jnp.logical_not(has_below))
    def _():
        volume[0:2] = zeros2

    @pl.when(jnp.logical_not(has_above))
    def _():
        volume[2 * slices + 2 :] = zeros2

    @pl.when(jnp.logical_not(has_before) & (side == 0))
    def _():
        volume[2 : 2 * slices + 2, 0:2] = zerosr

    @pl.when(jnp.logical_not(has_after) & (side == 1))
    def _():
        volume[2 : 2 * slices + 2, half + 2 : half + 4] = zerosr

    greet(wanted)

    def remote(source, target, slot, depth, light):
        return pltpu.make_async_remote_copy(
            src_ref=source,
            dst_ref=target,
            send_sem=send_sem.at[slot],
            recv_sem=recv_sem.at[slot],
            device_id=(depth, light),
            device_id_type=MESH,
        )

    swaps = []
    for part in range(2):
        two = slices // 2
        swaps.append(
            remote(
                viewed.at[pl.ds(part * two, two), pl.ds((half - 2) * (1 - side), half + 2)],
                volume.at[pl.ds(own + part * two, two), pl.ds(2 * side, half + 2)],
                part,
                other,
                light_at,
            )
        )
    swaps.append(
        remote(
            materials.at[:, pl.ds(half * (1 - side), half)], labels.at[pl.ds(slices * side, slices)], 2, other, light_at
        )
    )

    def to_after(sender):
        return volume.at[pl.ds(2 + slices * sender, slices), 0:2]

    def to_before(sender):
        return volume.at[pl.ds(2 + slices * sender, slices), half + 2 : half + 4]

    def rim(source, target, slot, depth, light):
        return pltpu.make_async_remote_copy(
            src_ref=source,
            dst_ref=target,
            send_sem=send_sem.at[slot],
            recv_sem=recv_sem.at[3 + side],
            device_id=(depth, light),
            device_id_type=MESH,
        )

    after_rim = rim(viewed.at[:, rows - 2 : rows], to_after(side), 3, even, light_at + 1)
    before_rim = rim(viewed.at[:, 0:2], to_before(side), 4, even + 1, light_at - 1)

    @pl.when(has_after)
    def _():
        after_rim.start()

    @pl.when(has_before)
    def _():
        before_rim.start()

    @pl.when(side == 0)
    def _():
        swaps[0].start()
        swaps[1].start()

    @pl.when(side == 1)
    def _():
        swaps[1].start()
        swaps[0].start()

    swaps[2].start()

    def rim_wait(sender):
        return pltpu.make_async_remote_copy(
            src_ref=to_after(sender),
            dst_ref=to_after(sender),
            send_sem=send_sem.at[3],
            recv_sem=recv_sem.at[3 + sender],
            device_id=(other, light_at),
            device_id_type=MESH,
        )

    @pl.when((has_before & (side == 0)) | (has_after & (side == 1)))
    def _():
        rim_wait(0).wait_recv()
        rim_wait(1).wait_recv()

    keep.wait()
    below = remote(volume.at[2:4], volume.at[2 * slices + 2 : 2 * slices + 4], 5, depth_at - 2, light_at)
    above = remote(volume.at[2 * slices : 2 * slices + 2], volume.at[0:2], 6, depth_at + 2, light_at)

    @pl.when((side == 0) & has_below)
    def _():
        below.start()

    @pl.when((side == 1) & has_above)
    def _():
        above.start()

    @pl.when(side == 0)
    def _():
        swaps[1].wait_recv()

    @pl.when(side == 1)
    def _():
        swaps[0].wait_recv()

    @pl.when((side == 1) & has_below)
    def _():
        below.start()

    @pl.when((side == 0) & has_above)
    def _():
        above.start()

    @pl.when(side == 0)
    def _():
        swaps[0].wait_recv()

    @pl.when(side == 1)
    def _():
        swaps[1].wait_recv()

    swaps[2].wait_recv()
    keep_labels.wait()

    @pl.when(has_above)
    def _():
        below.wait_recv()

    @pl.when(has_below)
    def _():
        above.wait_recv()

    for one in swaps:
        one.wait_send()

    @pl.when(has_below)
    def _():
        below.wait_send()

    @pl.when(has_above)
    def _():
        above.wait_send()

    @pl.when(has_after)
    def _():
        after_rim.wait_send()

    @pl.when(has_before)
    def _():
        before_rim.wait_send()


def trade(viewed, materials, depth_count, light_count):
    slices, rows = viewed.shape[:2]
    half = rows // 2
    return pl.pallas_call(
        functools.partial(trade_kernel, depth_count, light_count),
        in_specs=[VMEM_SPEC] * 2,
        out_specs=[VMEM_SPEC] * 2,
        out_shape=[
            jax.ShapeDtypeStruct((2 * slices + 4, half + 4, SUB, LANE), jnp.float32),
            jax.ShapeDtypeStruct((2 * slices, half, SUB, LANE), jnp.int32),
        ],
        scratch_shapes=[
            pltpu.SemaphoreType.DMA((2,)),
            pltpu.SemaphoreType.DMA((7,)),
            pltpu.SemaphoreType.DMA((7,)),
        ],
        compiler_params=pltpu.CompilerParams(
            collective_id=0, has_side_effects=True, vmem_limit_bytes=20 * 1024 * 1024
        ),
    )(viewed, materials)


def over_blend(front, back):
    through = 1.0 - front[3:4]
    return front + through * back


def merge_kernel(depth_count, light_count, plain, lit, through, image, blocks, *rest):
    stages = depth_count.bit_length() - 3
    taken = rest[:stages]
    ends, shadow, send_sem, recv_sem, end_send, end_recv, shadow_send, shadow_recv = rest[stages:]
    slices = through.shape[0]
    block_rows = blocks.shape[2]
    block_count = depth_count // 2
    stripes = 2 * light_count
    depth_at = lax.axis_index("depth")
    light_at = lax.axis_index("light")
    side = depth_at % 2
    pair = depth_at // 2
    stripe = light_at * 2 + side
    top = pair // (block_count // 2)
    low_bits = pair % (block_count // 2)

    def flipped(b):
        bit = (pair // (1 << b)) % 2
        return bit, (pair + (1 - 2 * bit) * (1 << b)) * 2 + side

    end_base = 2 * (side * (block_count // 2) + low_bits)
    source0 = 2 * low_bits + top
    source1 = 2 * (low_bits + block_count // 2) + top
    wanted = [(k != stripe, pair * 2 + k % 2, k // 2) for k in range(stripes)]
    wanted += [(depth_at >= 0, flipped(b)[1], light_at) for b in range(stages)]
    for x in range(2):
        wanted.append((end_base + x != depth_at, end_base + x, light_at))
    ends_from = [(source0 != depth_at, source0), (source1 != depth_at, source1)]
    wanted += [(exists, depth, light_at) for exists, depth in ends_from]
    greet(wanted)

    def shadow_copy(k, slot):
        return pltpu.make_async_remote_copy(
            src_ref=through,
            dst_ref=shadow.at[slot],
            send_sem=shadow_send.at[k],
            recv_sem=shadow_recv.at[slot],
            device_id=(pair * 2 + k % 2, k // 2),
            device_id_type=MESH,
        )

    for k in range(1, stripes):

        @pl.when(k > stripe)
        def _():
            shadow_copy(k, stripe).start()

    for z in range(slices):
        shadow[stripes, z] = jnp.ones((SUB, LANE), jnp.float32)
    for k in range(stripes - 1):

        @pl.when(k < stripe)
        def _():
            shadow_copy(k, k).wait_recv()
            for z in range(slices):
                shadow[stripes, z] = shadow[stripes, z] * shadow[k, z]

    lights = [shadow[stripes, z] for z in range(slices)]

    def finish(block):
        def one_row(i, carry):
            row = block * block_rows + i
            for c in range(3):
                value = plain[c, row]
                for z in range(slices):
                    value = value + lights[z] * lit[z * 3 + c, row]
                blocks[block, c, i] = value
            blocks[block, 3, i] = plain[3, row]
            return carry

        lax.fori_loop(0, block_rows, one_row, 0)

    def index_of(b, n, bit):
        uppers = block_count >> (b + 2)
        x, upper = n % 2, n // 2
        if uppers >= 2:
            later = (pair // (1 << (b + 1))) % 2
            rest = n % uppers
            x = rest % 2
            upper = 2 * (rest // 2) + (1 - later if n < uppers else later)
        return x + 2 * ((pair % (1 << b)) + (bit + 2 * upper) * (1 << b))

    def swap(b, n):
        bit, depth = flipped(b)
        slot = block_count - (block_count >> b) + n
        return pltpu.make_async_remote_copy(
            src_ref=blocks.at[index_of(b, n, 1 - bit)],
            dst_ref=taken[b].at[n],
            send_sem=send_sem.at[slot],
            recv_sem=recv_sem.at[slot],
            device_id=(depth, light_at),
            device_id_type=MESH,
        )

    count0 = block_count // 2
    bit0 = pair % 2
    for n in range(count0):
        finish(index_of(0, n, 1 - bit0))
        swap(0, n).start()
    for n in range(count0):
        finish(index_of(0, n, bit0))

    def blend_into(front_ref, back_ref, target_ref):
        for i in range(block_rows):
            clear = 1.0 - front_ref[3, i]
            for c in range(4):
                target_ref[c, i] = front_ref[c, i] + clear * back_ref[c, i]

    def blend(b, n):
        bit, depth = flipped(b)
        swap(b, n).wait_recv()
        mine = blocks.at[index_of(b, n, bit)]

        @pl.when(bit == 0)
        def _():
            blend_into(mine, taken[b].at[n], mine)

        @pl.when(bit == 1)
        def _():
            blend_into(taken[b].at[n], mine, mine)

    def end_copy(x, slot):
        return pltpu.make_async_remote_copy(
            src_ref=blocks.at[x + 2 * low_bits],
            dst_ref=ends.at[slot],
            send_sem=end_send.at[x],
            recv_sem=end_recv.at[slot],
            device_id=(end_base + x, light_at),
            device_id_type=MESH,
        )

    for b in range(stages):
        count = block_count >> (b + 1)
        bit, depth = flipped(b)
        if b + 1 < stages:
            for n in range(count // 2):
                blend(b, n)
            for n in range(count // 2):
                swap(b + 1, n).start()
            for n in range(count // 2, count):
                blend(b, n)
        else:
            for x in range(2):
                blend(b, x)

                @pl.when(end_base + x != depth_at)
                def _():
                    end_copy(x, top).start()

    stay = source0 == depth_at
    stay_late = source1 == depth_at
    mine = blocks.at[side + 2 * low_bits]

    @pl.when(jnp.logical_not(stay))
    def _():
        end_copy(0, 0).wait_recv()

    @pl.when(jnp.logical_not(stay_late))
    def _():
        end_copy(0, 1).wait_recv()

    @pl.when(stay)
    def _():
        blend_into(mine, ends.at[1], image)

    @pl.when(stay_late)
    def _():
        blend_into(ends.at[0], mine, image)

    @pl.when(jnp.logical_not(stay | stay_late))
    def _():
        blend_into(ends.at[0], ends.at[1], image)

    for b in range(stages):
        for n in range(block_count >> (b + 1)):
            swap(b, n).wait_send()
    for x in range(2):

        @pl.when(end_base + x != depth_at)
        def _():
            end_copy(x, top).wait_send()

    for k in range(1, stripes):

        @pl.when(k > stripe)
        def _():
            shadow_copy(k, stripe).wait_send()


def merge(plain, lit, through, depth_count, light_count):
    rows, slices = plain.shape[1], through.shape[0]
    f32 = jnp.float32
    block_count = depth_count // 2
    block = (4, rows // block_count, SUB, LANE)
    stages = depth_count.bit_length() - 3
    stripes = 2 * light_count
    dma = pltpu.SemaphoreType.DMA
    scratch = [pltpu.VMEM((block_count,) + block, f32)]
    scratch += [pltpu.VMEM((block_count >> (b + 1),) + block, f32) for b in range(stages)]
    scratch += [pltpu.VMEM((2,) + block, f32), pltpu.VMEM((stripes + 1, slices, SUB, LANE), f32)]
    scratch += [dma((block_count,)), dma((block_count,)), dma((2,)), dma((2,)), dma((stripes,)), dma((stripes,))]
    return pl.pallas_call(
        functools.partial(merge_kernel, depth_count, light_count),
        in_specs=[VMEM_SPEC] * 3,
        out_specs=VMEM_SPEC,
        out_shape=jax.ShapeDtypeStruct(block, f32),
        scratch_shapes=scratch,
        compiler_params=pltpu.CompilerParams(
            collective_id=1, has_side_effects=True, vmem_limit_bytes=40 * 1024 * 1024
        ),
    )(plain, lit, through)


def shards(density, labels, slice_order, extinction, albedo):
    depth_count = lax.axis_size("depth")
    light_count = lax.axis_size("light")
    slices, rows, columns = density.shape
    viewed, materials = reorder(density, labels, slice_order)
    volume, stripe_labels = trade(viewed, materials, depth_count, light_count)
    plain, lit, through = shade(volume, stripe_labels, extinction, albedo, depth_count, light_count)
    return merge(plain, lit, through, depth_count, light_count).reshape(4, -1)


def solution(mesh):
    return jax.shard_map(
        shards,
        mesh=mesh,
        in_specs=(P("depth", "light", None), P("depth", "light", None), P("depth"), P(), P()),
        out_specs=P(None, ("light", "depth")),
        check_vma=False,
    )
```

```python
import functools

import jax
import jax.numpy as jnp
from jax import lax
from jax.experimental import pallas as pl
from jax.experimental.pallas import tpu as pltpu
from jax.sharding import PartitionSpec as P

SUB, LANE = 8, 128
MESH = pl.DeviceIdType.MESH
VMEM_SPEC = pl.BlockSpec(memory_space=pltpu.VMEM)


def reorder_kernel(order, density, labels, viewed, materials, held, held_labels, sems):
    slices, rows = density.shape[:2]
    copies = []
    for source, target, base in ((density, held, 0), (labels, held_labels, slices)):
        for z in range(slices):
            at = lax.rem(order[z], slices)
            copies.append(pltpu.make_async_copy(source.at[at], target.at[z], sems.at[base + z]))
    for one in copies:
        one.start()
    for z in range(slices):
        copies[z].wait()
        viewed[z] = held[z].reshape(rows, SUB, LANE)
    for z in range(slices):
        copies[slices + z].wait()
        materials[z] = held_labels[z].reshape(rows, SUB, LANE)


def reorder(density, labels, order):
    slices, rows, columns = density.shape
    shape = (slices, rows, SUB, LANE)
    far = pl.BlockSpec(memory_space=pltpu.HBM)
    return pl.pallas_call(
        reorder_kernel,
        in_specs=[pl.BlockSpec(memory_space=pltpu.SMEM), far, far],
        out_specs=[VMEM_SPEC] * 2,
        out_shape=[
            jax.ShapeDtypeStruct(shape, density.dtype),
            jax.ShapeDtypeStruct(shape, labels.dtype),
        ],
        scratch_shapes=[
            pltpu.VMEM(density.shape, density.dtype),
            pltpu.VMEM(labels.shape, labels.dtype),
            pltpu.SemaphoreType.DMA((2 * slices,)),
        ],
        compiler_params=pltpu.CompilerParams(vmem_limit_bytes=12 * 1024 * 1024),
    )(order, density, labels)


def beside_y(cells, lane, first, last):
    low = pltpu.roll(cells, 1, 1)
    high = pltpu.roll(cells, LANE - 1, 1)
    low = jnp.where(lane == 0, pltpu.roll(low, 1, 0), low)
    high = jnp.where(lane == LANE - 1, pltpu.roll(high, SUB - 1, 0), high)
    return jnp.where(first, 0.0, low), jnp.where(last, 0.0, high)


def lookup(table, index):
    return jnp.take_along_axis(table, index, axis=1, mode="promise_in_bounds")


def shade_kernel(heat, turned, labels, extinction, albedo, plain, lit, through):
    slices, rows = labels.shape[:2]
    lane = lax.broadcasted_iota(jnp.int32, (SUB, LANE), 1)
    tables = [jnp.zeros((SUB, LANE), jnp.float32) for _ in range(4)]
    for k in range(extinction.shape[0]):
        tables[0] = jnp.where(lane == k, extinction[k], tables[0])
        for c in range(3):
            tables[c + 1] = jnp.where(lane == k, albedo[c, k], tables[c + 1])
    def shade_row(r, lights):
        lights = list(lights)
        remaining = jnp.ones((SUB, LANE), jnp.float32)
        flat = [jnp.zeros((SUB, LANE), jnp.float32) for _ in range(3)]
        for z in range(slices):
            index = labels[z, r]
            optical = lookup(tables[0], index) * heat[z, r]
            passed = jnp.exp(-optical)
            weight = (1.0 - passed) * remaining
            glow = weight * lights[z] * turned[z, r]
            faint = 0.2 * weight
            for c in range(3):
                tint = lookup(tables[c + 1], index)
                flat[c] = flat[c] + tint * faint
                lit[z * 3 + c, r] = tint * glow
            remaining = remaining * passed
            lights[z] = lights[z] * passed
        for c in range(3):
            plain[c, r] = flat[c]
        plain[3, r] = 1.0 - remaining
        return tuple(lights)

    ones = tuple(jnp.ones((SUB, LANE), jnp.float32) for _ in range(slices))
    lights = lax.fori_loop(0, rows, shade_row, ones)
    for z in range(slices):
        through[z] = lights[z]


def shade(heat, turned, labels, extinction, albedo):
    slices, rows = labels.shape[:2]
    f32 = jnp.float32
    return pl.pallas_call(
        shade_kernel,
        in_specs=[VMEM_SPEC] * 3 + [pl.BlockSpec(memory_space=pltpu.SMEM)] * 2,
        out_specs=[VMEM_SPEC] * 3,
        out_shape=[
            jax.ShapeDtypeStruct((4, rows, SUB, LANE), f32),
            jax.ShapeDtypeStruct((slices * 3, rows, SUB, LANE), f32),
            jax.ShapeDtypeStruct((slices, SUB, LANE), f32),
        ],
        compiler_params=pltpu.CompilerParams(vmem_limit_bytes=40 * 1024 * 1024),
    )(heat, turned, labels, extinction, albedo)


def greet(wanted):
    barrier = pltpu.get_barrier_semaphore()
    count = 0
    for exists, depth, light in wanted:

        @pl.when(exists)
        def _():
            pl.semaphore_signal(barrier, inc=1, device_id=(depth, light), device_id_type=MESH)

        count = count + jnp.where(exists, 1, 0)
    pl.semaphore_wait(barrier, count)


def slopes(volume, smooth, heat, turned, flags):
    slices, rows = heat.shape[:2]
    lane = lax.broadcasted_iota(jnp.int32, (SUB, LANE), 1)
    sub = lax.broadcasted_iota(jnp.int32, (SUB, LANE), 0)
    first = (lane == 0) & (sub == 0)
    last = (lane == LANE - 1) & (sub == SUB - 1)

    def smooth_row(i, carry):
        column = [volume[z, i + 1] for z in range(slices + 4)]
        for z in range(slices + 2):
            center = column[z + 1]
            low, high = beside_y(center, lane, first, last)
            total = (column[z] + column[z + 2]) + (volume[z + 1, i] + volume[z + 1, i + 2]) + (low + high)
            value = 0.4 * center + 0.1 * total
            if z == 0:
                value = value * flags[0]
            if z == slices + 1:
                value = value * flags[1]
            smooth[z, i] = value
        return carry

    lax.fori_loop(0, rows + 2, smooth_row, 0)
    for z in range(slices):
        smooth[z + 1, 0] = smooth[z + 1, 0] * flags[2]
        smooth[z + 1, rows + 1] = smooth[z + 1, rows + 1] * flags[3]

    def slope_row(r, carry):
        for z in range(slices):
            center = smooth[z + 1, r + 1]
            low, high = beside_y(center, lane, first, last)
            grad_z = smooth[z + 2, r + 1] - smooth[z, r + 1]
            grad_x = smooth[z + 1, r + 2] - smooth[z + 1, r]
            grad_y = high - low
            facing = grad_x * lax.rsqrt(grad_z * grad_z + grad_x * grad_x + grad_y * grad_y + 0.2)
            heat[z, r] = jnp.exp(center)
            turned[z, r] = 0.5 + 0.5 * facing
        return carry

    lax.fori_loop(0, rows, slope_row, 0)


def trade_kernel(depth_count, light_count, viewed, materials, heat, turned, labels, volume, smooth, local_sem, send_sem, recv_sem):
    slices, rows = viewed.shape[:2]
    half = rows // 2
    depth_at = lax.axis_index("depth")
    light_at = lax.axis_index("light")
    side = depth_at % 2
    pair = depth_at // 2
    even = pair * 2
    other = even + 1 - side
    has_below = pair > 0
    has_above = pair < depth_count // 2 - 1
    has_before = light_at > 0
    has_after = light_at < light_count - 1
    own = 2 + slices * side
    wanted = [(depth_at >= 0, other, light_at)]
    for exists, light in ((has_before, light_at - 1), (has_after, light_at + 1)):
        wanted += [(exists, even, light), (exists, even + 1, light)]
    wanted += [(has_below, depth_at - 2, light_at), (has_above, depth_at + 2, light_at)]

    def piece(to_side):
        return viewed.at[:, pl.ds((half - 2) * to_side, half + 2)]

    def spot(from_side, to_side):
        return volume.at[pl.ds(2 + slices * from_side, slices), pl.ds(2 - 2 * to_side, half + 2)]

    keep = pltpu.make_async_copy(piece(side), spot(side, side), local_sem.at[0])
    keep_labels = pltpu.make_async_copy(
        materials.at[:, pl.ds(half * side, half)], labels.at[pl.ds(slices * side, slices)], local_sem.at[1]
    )
    keep.start()
    keep_labels.start()
    zeros2 = jnp.zeros((2, half + 4, SUB, LANE), jnp.float32)
    zerosr = jnp.zeros((volume.shape[0] - 4, 2, SUB, LANE), jnp.float32)

    @pl.when(jnp.logical_not(has_below))
    def _():
        volume[0:2] = zeros2

    @pl.when(jnp.logical_not(has_above))
    def _():
        volume[2 * slices + 2 :] = zeros2

    @pl.when(jnp.logical_not(has_before) & (side == 0))
    def _():
        volume[2 : 2 * slices + 2, 0:2] = zerosr

    @pl.when(jnp.logical_not(has_after) & (side == 1))
    def _():
        volume[2 : 2 * slices + 2, half + 2 : half + 4] = zerosr

    greet(wanted)

    def remote(source, target, slot, depth, light):
        return pltpu.make_async_remote_copy(
            src_ref=source,
            dst_ref=target,
            send_sem=send_sem.at[slot],
            recv_sem=recv_sem.at[slot],
            device_id=(depth, light),
            device_id_type=MESH,
        )

    swaps = []
    for part in range(2):
        two = slices // 2
        swaps.append(
            remote(
                viewed.at[pl.ds(part * two, two), pl.ds((half - 2) * (1 - side), half + 2)],
                volume.at[pl.ds(own + part * two, two), pl.ds(2 * side, half + 2)],
                part,
                other,
                light_at,
            )
        )
    swaps.append(
        remote(
            materials.at[:, pl.ds(half * (1 - side), half)], labels.at[pl.ds(slices * side, slices)], 2, other, light_at
        )
    )

    def to_after(sender):
        return volume.at[pl.ds(2 + slices * sender, slices), 0:2]

    def to_before(sender):
        return volume.at[pl.ds(2 + slices * sender, slices), half + 2 : half + 4]

    def rim(source, target, slot, depth, light):
        return pltpu.make_async_remote_copy(
            src_ref=source,
            dst_ref=target,
            send_sem=send_sem.at[slot],
            recv_sem=recv_sem.at[3 + side],
            device_id=(depth, light),
            device_id_type=MESH,
        )

    after_rim = rim(viewed.at[:, rows - 2 : rows], to_after(side), 3, even, light_at + 1)
    before_rim = rim(viewed.at[:, 0:2], to_before(side), 4, even + 1, light_at - 1)

    @pl.when(has_after)
    def _():
        after_rim.start()

    @pl.when(has_before)
    def _():
        before_rim.start()

    @pl.when(side == 0)
    def _():
        swaps[0].start()
        swaps[1].start()

    @pl.when(side == 1)
    def _():
        swaps[1].start()
        swaps[0].start()

    swaps[2].start()

    def rim_wait(sender):
        return pltpu.make_async_remote_copy(
            src_ref=to_after(sender),
            dst_ref=to_after(sender),
            send_sem=send_sem.at[3],
            recv_sem=recv_sem.at[3 + sender],
            device_id=(other, light_at),
            device_id_type=MESH,
        )

    @pl.when((has_before & (side == 0)) | (has_after & (side == 1)))
    def _():
        rim_wait(0).wait_recv()
        rim_wait(1).wait_recv()

    keep.wait()
    below = remote(volume.at[2:4], volume.at[2 * slices + 2 : 2 * slices + 4], 5, depth_at - 2, light_at)
    above = remote(volume.at[2 * slices : 2 * slices + 2], volume.at[0:2], 6, depth_at + 2, light_at)

    @pl.when((side == 0) & has_below)
    def _():
        below.start()

    @pl.when((side == 1) & has_above)
    def _():
        above.start()

    @pl.when(side == 0)
    def _():
        swaps[1].wait_recv()

    @pl.when(side == 1)
    def _():
        swaps[0].wait_recv()

    @pl.when((side == 1) & has_below)
    def _():
        below.start()

    @pl.when((side == 0) & has_above)
    def _():
        above.start()

    @pl.when(side == 0)
    def _():
        swaps[0].wait_recv()

    @pl.when(side == 1)
    def _():
        swaps[1].wait_recv()

    @pl.when(has_above)
    def _():
        below.wait_recv()

    @pl.when(has_below)
    def _():
        above.wait_recv()

    stripe = light_at * 2 + side
    flags = [has_below, has_above, stripe > 0, stripe < 2 * light_count - 1]
    slopes(volume, smooth, heat, turned, [jnp.where(flag, 1.0, 0.0) for flag in flags])
    swaps[2].wait_recv()
    keep_labels.wait()

    for one in swaps:
        one.wait_send()

    @pl.when(has_below)
    def _():
        below.wait_send()

    @pl.when(has_above)
    def _():
        above.wait_send()

    @pl.when(has_after)
    def _():
        after_rim.wait_send()

    @pl.when(has_before)
    def _():
        before_rim.wait_send()


def trade(viewed, materials, depth_count, light_count):
    slices, rows = viewed.shape[:2]
    half = rows // 2
    return pl.pallas_call(
        functools.partial(trade_kernel, depth_count, light_count),
        in_specs=[VMEM_SPEC] * 2,
        out_specs=[VMEM_SPEC] * 3,
        out_shape=[
            jax.ShapeDtypeStruct((2 * slices, half, SUB, LANE), jnp.float32),
            jax.ShapeDtypeStruct((2 * slices, half, SUB, LANE), jnp.float32),
            jax.ShapeDtypeStruct((2 * slices, half, SUB, LANE), jnp.int32),
        ],
        scratch_shapes=[
            pltpu.VMEM((2 * slices + 4, half + 4, SUB, LANE), jnp.float32),
            pltpu.VMEM((2 * slices + 2, half + 2, SUB, LANE), jnp.float32),
            pltpu.SemaphoreType.DMA((2,)),
            pltpu.SemaphoreType.DMA((7,)),
            pltpu.SemaphoreType.DMA((7,)),
        ],
        compiler_params=pltpu.CompilerParams(
            collective_id=0, has_side_effects=True, vmem_limit_bytes=20 * 1024 * 1024
        ),
    )(viewed, materials)


def over_blend(front, back):
    through = 1.0 - front[3:4]
    return front + through * back


def merge_kernel(depth_count, light_count, plain, lit, through, image, blocks, *rest):
    stages = depth_count.bit_length() - 3
    taken = rest[:stages]
    ends, shadow, send_sem, recv_sem, end_send, end_recv, shadow_send, shadow_recv = rest[stages:]
    slices = through.shape[0]
    block_rows = blocks.shape[2]
    block_count = depth_count // 2
    stripes = 2 * light_count
    depth_at = lax.axis_index("depth")
    light_at = lax.axis_index("light")
    side = depth_at % 2
    pair = depth_at // 2
    stripe = light_at * 2 + side
    top = pair // (block_count // 2)
    low_bits = pair % (block_count // 2)

    def flipped(b):
        bit = (pair // (1 << b)) % 2
        return bit, (pair + (1 - 2 * bit) * (1 << b)) * 2 + side

    end_base = 2 * (side * (block_count // 2) + low_bits)
    source0 = 2 * low_bits + top
    source1 = 2 * (low_bits + block_count // 2) + top
    wanted = [(k != stripe, pair * 2 + k % 2, k // 2) for k in range(stripes)]
    wanted += [(depth_at >= 0, flipped(b)[1], light_at) for b in range(stages)]
    for x in range(2):
        wanted.append((end_base + x != depth_at, end_base + x, light_at))
    ends_from = [(source0 != depth_at, source0), (source1 != depth_at, source1)]
    wanted += [(exists, depth, light_at) for exists, depth in ends_from]
    greet(wanted)

    def shadow_copy(k, slot):
        return pltpu.make_async_remote_copy(
            src_ref=through,
            dst_ref=shadow.at[slot],
            send_sem=shadow_send.at[k],
            recv_sem=shadow_recv.at[slot],
            device_id=(pair * 2 + k % 2, k // 2),
            device_id_type=MESH,
        )

    for k in range(1, stripes):

        @pl.when(k > stripe)
        def _():
            shadow_copy(k, stripe).start()

    for z in range(slices):
        shadow[stripes, z] = jnp.ones((SUB, LANE), jnp.float32)
    for k in range(stripes - 1):

        @pl.when(k < stripe)
        def _():
            shadow_copy(k, k).wait_recv()
            for z in range(slices):
                shadow[stripes, z] = shadow[stripes, z] * shadow[k, z]

    lights = [shadow[stripes, z] for z in range(slices)]

    def finish(block):
        def one_row(i, carry):
            row = block * block_rows + i
            for c in range(3):
                value = plain[c, row]
                for z in range(slices):
                    value = value + lights[z] * lit[z * 3 + c, row]
                blocks[block, c, i] = value
            blocks[block, 3, i] = plain[3, row]
            return carry

        lax.fori_loop(0, block_rows, one_row, 0)

    def index_of(b, n, bit):
        uppers = block_count >> (b + 2)
        x, upper = n % 2, n // 2
        if uppers >= 2:
            later = (pair // (1 << (b + 1))) % 2
            rest = n % uppers
            x = rest % 2
            upper = 2 * (rest // 2) + (1 - later if n < uppers else later)
        return x + 2 * ((pair % (1 << b)) + (bit + 2 * upper) * (1 << b))

    def swap(b, n):
        bit, depth = flipped(b)
        slot = block_count - (block_count >> b) + n
        return pltpu.make_async_remote_copy(
            src_ref=blocks.at[index_of(b, n, 1 - bit)],
            dst_ref=taken[b].at[n],
            send_sem=send_sem.at[slot],
            recv_sem=recv_sem.at[slot],
            device_id=(depth, light_at),
            device_id_type=MESH,
        )

    count0 = block_count // 2
    bit0 = pair % 2
    for n in range(count0):
        finish(index_of(0, n, 1 - bit0))
        swap(0, n).start()
    for n in range(count0):
        finish(index_of(0, n, bit0))

    def blend_into(front_ref, back_ref, target_ref):
        for i in range(block_rows):
            clear = 1.0 - front_ref[3, i]
            for c in range(4):
                target_ref[c, i] = front_ref[c, i] + clear * back_ref[c, i]

    def blend(b, n):
        bit, depth = flipped(b)
        swap(b, n).wait_recv()
        mine = blocks.at[index_of(b, n, bit)]

        @pl.when(bit == 0)
        def _():
            blend_into(mine, taken[b].at[n], mine)

        @pl.when(bit == 1)
        def _():
            blend_into(taken[b].at[n], mine, mine)

    def end_copy(x, slot):
        return pltpu.make_async_remote_copy(
            src_ref=blocks.at[x + 2 * low_bits],
            dst_ref=ends.at[slot],
            send_sem=end_send.at[x],
            recv_sem=end_recv.at[slot],
            device_id=(end_base + x, light_at),
            device_id_type=MESH,
        )

    for b in range(stages):
        count = block_count >> (b + 1)
        bit, depth = flipped(b)
        if b + 1 < stages:
            for n in range(count // 2):
                blend(b, n)
            for n in range(count // 2):
                swap(b + 1, n).start()
            for n in range(count // 2, count):
                blend(b, n)
        else:
            for x in range(2):
                blend(b, x)

                @pl.when(end_base + x != depth_at)
                def _():
                    end_copy(x, top).start()

    stay = source0 == depth_at
    stay_late = source1 == depth_at
    mine = blocks.at[side + 2 * low_bits]

    @pl.when(jnp.logical_not(stay))
    def _():
        end_copy(0, 0).wait_recv()

    @pl.when(jnp.logical_not(stay_late))
    def _():
        end_copy(0, 1).wait_recv()

    @pl.when(stay)
    def _():
        blend_into(mine, ends.at[1], image)

    @pl.when(stay_late)
    def _():
        blend_into(ends.at[0], mine, image)

    @pl.when(jnp.logical_not(stay | stay_late))
    def _():
        blend_into(ends.at[0], ends.at[1], image)

    for b in range(stages):
        for n in range(block_count >> (b + 1)):
            swap(b, n).wait_send()
    for x in range(2):

        @pl.when(end_base + x != depth_at)
        def _():
            end_copy(x, top).wait_send()

    for k in range(1, stripes):

        @pl.when(k > stripe)
        def _():
            shadow_copy(k, stripe).wait_send()


def merge(plain, lit, through, depth_count, light_count):
    rows, slices = plain.shape[1], through.shape[0]
    f32 = jnp.float32
    block_count = depth_count // 2
    block = (4, rows // block_count, SUB, LANE)
    stages = depth_count.bit_length() - 3
    stripes = 2 * light_count
    dma = pltpu.SemaphoreType.DMA
    scratch = [pltpu.VMEM((block_count,) + block, f32)]
    scratch += [pltpu.VMEM((block_count >> (b + 1),) + block, f32) for b in range(stages)]
    scratch += [pltpu.VMEM((2,) + block, f32), pltpu.VMEM((stripes + 1, slices, SUB, LANE), f32)]
    scratch += [dma((block_count,)), dma((block_count,)), dma((2,)), dma((2,)), dma((stripes,)), dma((stripes,))]
    return pl.pallas_call(
        functools.partial(merge_kernel, depth_count, light_count),
        in_specs=[VMEM_SPEC] * 3,
        out_specs=VMEM_SPEC,
        out_shape=jax.ShapeDtypeStruct(block, f32),
        scratch_shapes=scratch,
        compiler_params=pltpu.CompilerParams(
            collective_id=1, has_side_effects=True, vmem_limit_bytes=40 * 1024 * 1024
        ),
    )(plain, lit, through)


def shards(density, labels, slice_order, extinction, albedo):
    depth_count = lax.axis_size("depth")
    light_count = lax.axis_size("light")
    slices, rows, columns = density.shape
    viewed, materials = reorder(density, labels, slice_order)
    heat, turned, stripe_labels = trade(viewed, materials, depth_count, light_count)
    plain, lit, through = shade(heat, turned, stripe_labels, extinction, albedo)
    return merge(plain, lit, through, depth_count, light_count).reshape(4, -1)


def solution(mesh):
    return jax.shard_map(
        shards,
        mesh=mesh,
        in_specs=(P("depth", "light", None), P("depth", "light", None), P("depth"), P(), P()),
        out_specs=P(None, ("light", "depth")),
        check_vma=False,
    )
```

```python
import functools

import jax
import jax.numpy as jnp
from jax import lax
from jax.experimental import pallas as pl
from jax.experimental.pallas import tpu as pltpu
from jax.sharding import PartitionSpec as P

SUB, LANE = 8, 128
MESH = pl.DeviceIdType.MESH
VMEM_SPEC = pl.BlockSpec(memory_space=pltpu.VMEM)


def reorder_kernel(order, density, labels, viewed, materials, held, held_labels, sems):
    slices, rows = density.shape[:2]
    copies = []
    for source, target, base in ((density, held, 0), (labels, held_labels, slices)):
        for z in range(slices):
            at = lax.rem(order[z], slices)
            copies.append(pltpu.make_async_copy(source.at[at], target.at[z], sems.at[base + z]))
    for one in copies:
        one.start()
    for z in range(slices):
        copies[z].wait()
        viewed[z] = held[z].reshape(rows, SUB, LANE)
    for z in range(slices):
        copies[slices + z].wait()
        materials[z] = held_labels[z].reshape(rows, SUB, LANE)


def reorder(density, labels, order):
    slices, rows, columns = density.shape
    shape = (slices, rows, SUB, LANE)
    far = pl.BlockSpec(memory_space=pltpu.HBM)
    return pl.pallas_call(
        reorder_kernel,
        in_specs=[pl.BlockSpec(memory_space=pltpu.SMEM), far, far],
        out_specs=[VMEM_SPEC] * 2,
        out_shape=[
            jax.ShapeDtypeStruct(shape, density.dtype),
            jax.ShapeDtypeStruct(shape, labels.dtype),
        ],
        scratch_shapes=[
            pltpu.VMEM(density.shape, density.dtype),
            pltpu.VMEM(labels.shape, labels.dtype),
            pltpu.SemaphoreType.DMA((2 * slices,)),
        ],
        compiler_params=pltpu.CompilerParams(vmem_limit_bytes=12 * 1024 * 1024),
    )(
        order,
        pltpu.with_memory_space_constraint(density, pltpu.HBM),
        pltpu.with_memory_space_constraint(labels, pltpu.HBM),
    )


def beside_y(cells, lane, first, last):
    low = pltpu.roll(cells, 1, 1)
    high = pltpu.roll(cells, LANE - 1, 1)
    low = jnp.where(lane == 0, pltpu.roll(low, 1, 0), low)
    high = jnp.where(lane == LANE - 1, pltpu.roll(high, SUB - 1, 0), high)
    return jnp.where(first, 0.0, low), jnp.where(last, 0.0, high)


def lookup(table, index):
    return jnp.take_along_axis(table, index, axis=1, mode="promise_in_bounds")


def shade_kernel(heat, turned, labels, extinction, albedo, plain, lit, through):
    slices, rows = labels.shape[:2]
    lane = lax.broadcasted_iota(jnp.int32, (SUB, LANE), 1)
    tables = [jnp.zeros((SUB, LANE), jnp.float32) for _ in range(4)]
    for k in range(extinction.shape[0]):
        tables[0] = jnp.where(lane == k, extinction[k], tables[0])
        for c in range(3):
            tables[c + 1] = jnp.where(lane == k, albedo[c, k], tables[c + 1])
    def shade_row(r, lights):
        lights = list(lights)
        remaining = jnp.ones((SUB, LANE), jnp.float32)
        flat = [jnp.zeros((SUB, LANE), jnp.float32) for _ in range(3)]
        for z in range(slices):
            index = labels[z, r]
            optical = lookup(tables[0], index) * heat[z, r]
            passed = jnp.exp(-optical)
            weight = (1.0 - passed) * remaining
            glow = weight * lights[z] * turned[z, r]
            faint = 0.2 * weight
            for c in range(3):
                tint = lookup(tables[c + 1], index)
                flat[c] = flat[c] + tint * faint
                lit[z * 3 + c, r] = tint * glow
            remaining = remaining * passed
            lights[z] = lights[z] * passed
        for c in range(3):
            plain[c, r] = flat[c]
        plain[3, r] = 1.0 - remaining
        return tuple(lights)

    ones = tuple(jnp.ones((SUB, LANE), jnp.float32) for _ in range(slices))
    lights = lax.fori_loop(0, rows, shade_row, ones)
    for z in range(slices):
        through[z] = lights[z]


def shade(heat, turned, labels, extinction, albedo):
    slices, rows = labels.shape[:2]
    f32 = jnp.float32
    return pl.pallas_call(
        shade_kernel,
        in_specs=[VMEM_SPEC] * 3 + [pl.BlockSpec(memory_space=pltpu.SMEM)] * 2,
        out_specs=[VMEM_SPEC] * 3,
        out_shape=[
            jax.ShapeDtypeStruct((4, rows, SUB, LANE), f32),
            jax.ShapeDtypeStruct((slices * 3, rows, SUB, LANE), f32),
            jax.ShapeDtypeStruct((slices, SUB, LANE), f32),
        ],
        compiler_params=pltpu.CompilerParams(vmem_limit_bytes=40 * 1024 * 1024),
    )(heat, turned, labels, extinction, albedo)


def greet(wanted):
    barrier = pltpu.get_barrier_semaphore()
    count = 0
    for exists, depth, light in wanted:

        @pl.when(exists)
        def _():
            pl.semaphore_signal(barrier, inc=1, device_id=(depth, light), device_id_type=MESH)

        count = count + jnp.where(exists, 1, 0)
    pl.semaphore_wait(barrier, count)


def slopes(volume, smooth, heat, turned, flags):
    slices, rows = heat.shape[:2]
    lane = lax.broadcasted_iota(jnp.int32, (SUB, LANE), 1)
    sub = lax.broadcasted_iota(jnp.int32, (SUB, LANE), 0)
    first = (lane == 0) & (sub == 0)
    last = (lane == LANE - 1) & (sub == SUB - 1)

    def smooth_row(i, carry):
        column = [volume[z, i + 1] for z in range(slices + 4)]
        for z in range(slices + 2):
            center = column[z + 1]
            low, high = beside_y(center, lane, first, last)
            total = (column[z] + column[z + 2]) + (volume[z + 1, i] + volume[z + 1, i + 2]) + (low + high)
            value = 0.4 * center + 0.1 * total
            if z == 0:
                value = value * flags[0]
            if z == slices + 1:
                value = value * flags[1]
            smooth[z, i] = value
        return carry

    lax.fori_loop(0, rows + 2, smooth_row, 0)
    for z in range(slices):
        smooth[z + 1, 0] = smooth[z + 1, 0] * flags[2]
        smooth[z + 1, rows + 1] = smooth[z + 1, rows + 1] * flags[3]

    def slope_row(r, carry):
        for z in range(slices):
            center = smooth[z + 1, r + 1]
            low, high = beside_y(center, lane, first, last)
            grad_z = smooth[z + 2, r + 1] - smooth[z, r + 1]
            grad_x = smooth[z + 1, r + 2] - smooth[z + 1, r]
            grad_y = high - low
            facing = grad_x * lax.rsqrt(grad_z * grad_z + grad_x * grad_x + grad_y * grad_y + 0.2)
            heat[z, r] = jnp.exp(center)
            turned[z, r] = 0.5 + 0.5 * facing
        return carry

    lax.fori_loop(0, rows, slope_row, 0)


def trade_kernel(depth_count, light_count, viewed, materials, heat, turned, labels, volume, smooth, local_sem, send_sem, recv_sem):
    slices, rows = viewed.shape[:2]
    half = rows // 2
    depth_at = lax.axis_index("depth")
    light_at = lax.axis_index("light")
    side = depth_at % 2
    pair = depth_at // 2
    even = pair * 2
    other = even + 1 - side
    has_below = pair > 0
    has_above = pair < depth_count // 2 - 1
    has_before = light_at > 0
    has_after = light_at < light_count - 1
    own = 2 + slices * side
    wanted = [(depth_at >= 0, other, light_at)]
    for exists, light in ((has_before, light_at - 1), (has_after, light_at + 1)):
        wanted += [(exists, even, light), (exists, even + 1, light)]
    wanted += [(has_below, depth_at - 2, light_at), (has_above, depth_at + 2, light_at)]

    def piece(to_side):
        return viewed.at[:, pl.ds((half - 2) * to_side, half + 2)]

    def spot(from_side, to_side):
        return volume.at[pl.ds(2 + slices * from_side, slices), pl.ds(2 - 2 * to_side, half + 2)]

    keep = pltpu.make_async_copy(piece(side), spot(side, side), local_sem.at[0])
    keep_labels = pltpu.make_async_copy(
        materials.at[:, pl.ds(half * side, half)], labels.at[pl.ds(slices * side, slices)], local_sem.at[1]
    )
    keep.start()
    keep_labels.start()
    zeros2 = jnp.zeros((2, half + 4, SUB, LANE), jnp.float32)
    zerosr = jnp.zeros((volume.shape[0] - 4, 2, SUB, LANE), jnp.float32)

    @pl.when(jnp.logical_not(has_below))
    def _():
        volume[0:2] = zeros2

    @pl.when(jnp.logical_not(has_above))
    def _():
        volume[2 * slices + 2 :] = zeros2

    @pl.when(jnp.logical_not(has_before) & (side == 0))
    def _():
        volume[2 : 2 * slices + 2, 0:2] = zerosr

    @pl.when(jnp.logical_not(has_after) & (side == 1))
    def _():
        volume[2 : 2 * slices + 2, half + 2 : half + 4] = zerosr

    greet(wanted)

    def remote(source, target, slot, depth, light):
        return pltpu.make_async_remote_copy(
            src_ref=source,
            dst_ref=target,
            send_sem=send_sem.at[slot],
            recv_sem=recv_sem.at[slot],
            device_id=(depth, light),
            device_id_type=MESH,
        )

    swaps = []
    for part in range(2):
        two = slices // 2
        swaps.append(
            remote(
                viewed.at[pl.ds(part * two, two), pl.ds((half - 2) * (1 - side), half + 2)],
                volume.at[pl.ds(own + part * two, two), pl.ds(2 * side, half + 2)],
                part,
                other,
                light_at,
            )
        )
    swaps.append(
        remote(
            materials.at[:, pl.ds(half * (1 - side), half)], labels.at[pl.ds(slices * side, slices)], 2, other, light_at
        )
    )

    def to_after(sender):
        return volume.at[pl.ds(2 + slices * sender, slices), 0:2]

    def to_before(sender):
        return volume.at[pl.ds(2 + slices * sender, slices), half + 2 : half + 4]

    def rim(source, target, slot, depth, light):
        return pltpu.make_async_remote_copy(
            src_ref=source,
            dst_ref=target,
            send_sem=send_sem.at[slot],
            recv_sem=recv_sem.at[3 + side],
            device_id=(depth, light),
            device_id_type=MESH,
        )

    after_rim = rim(viewed.at[:, rows - 2 : rows], to_after(side), 3, even, light_at + 1)
    before_rim = rim(viewed.at[:, 0:2], to_before(side), 4, even + 1, light_at - 1)

    @pl.when(has_after)
    def _():
        after_rim.start()

    @pl.when(has_before)
    def _():
        before_rim.start()

    @pl.when(side == 0)
    def _():
        swaps[0].start()
        swaps[1].start()

    @pl.when(side == 1)
    def _():
        swaps[1].start()
        swaps[0].start()

    swaps[2].start()

    def rim_wait(sender):
        return pltpu.make_async_remote_copy(
            src_ref=to_after(sender),
            dst_ref=to_after(sender),
            send_sem=send_sem.at[3],
            recv_sem=recv_sem.at[3 + sender],
            device_id=(other, light_at),
            device_id_type=MESH,
        )

    @pl.when((has_before & (side == 0)) | (has_after & (side == 1)))
    def _():
        rim_wait(0).wait_recv()
        rim_wait(1).wait_recv()

    keep.wait()
    below = remote(volume.at[2:4], volume.at[2 * slices + 2 : 2 * slices + 4], 5, depth_at - 2, light_at)
    above = remote(volume.at[2 * slices : 2 * slices + 2], volume.at[0:2], 6, depth_at + 2, light_at)

    @pl.when((side == 0) & has_below)
    def _():
        below.start()

    @pl.when((side == 1) & has_above)
    def _():
        above.start()

    @pl.when(side == 0)
    def _():
        swaps[1].wait_recv()

    @pl.when(side == 1)
    def _():
        swaps[0].wait_recv()

    @pl.when((side == 1) & has_below)
    def _():
        below.start()

    @pl.when((side == 0) & has_above)
    def _():
        above.start()

    @pl.when(side == 0)
    def _():
        swaps[0].wait_recv()

    @pl.when(side == 1)
    def _():
        swaps[1].wait_recv()

    @pl.when(has_above)
    def _():
        below.wait_recv()

    @pl.when(has_below)
    def _():
        above.wait_recv()

    stripe = light_at * 2 + side
    flags = [has_below, has_above, stripe > 0, stripe < 2 * light_count - 1]
    slopes(volume, smooth, heat, turned, [jnp.where(flag, 1.0, 0.0) for flag in flags])
    swaps[2].wait_recv()
    keep_labels.wait()

    for one in swaps:
        one.wait_send()

    @pl.when(has_below)
    def _():
        below.wait_send()

    @pl.when(has_above)
    def _():
        above.wait_send()

    @pl.when(has_after)
    def _():
        after_rim.wait_send()

    @pl.when(has_before)
    def _():
        before_rim.wait_send()


def trade(viewed, materials, depth_count, light_count):
    slices, rows = viewed.shape[:2]
    half = rows // 2
    return pl.pallas_call(
        functools.partial(trade_kernel, depth_count, light_count),
        in_specs=[VMEM_SPEC] * 2,
        out_specs=[VMEM_SPEC] * 3,
        out_shape=[
            jax.ShapeDtypeStruct((2 * slices, half, SUB, LANE), jnp.float32),
            jax.ShapeDtypeStruct((2 * slices, half, SUB, LANE), jnp.float32),
            jax.ShapeDtypeStruct((2 * slices, half, SUB, LANE), jnp.int32),
        ],
        scratch_shapes=[
            pltpu.VMEM((2 * slices + 4, half + 4, SUB, LANE), jnp.float32),
            pltpu.VMEM((2 * slices + 2, half + 2, SUB, LANE), jnp.float32),
            pltpu.SemaphoreType.DMA((2,)),
            pltpu.SemaphoreType.DMA((7,)),
            pltpu.SemaphoreType.DMA((7,)),
        ],
        compiler_params=pltpu.CompilerParams(
            collective_id=0, has_side_effects=True, vmem_limit_bytes=20 * 1024 * 1024
        ),
    )(viewed, materials)


def over_blend(front, back):
    through = 1.0 - front[3:4]
    return front + through * back


def merge_kernel(depth_count, light_count, plain, lit, through, image, blocks, *rest):
    stages = depth_count.bit_length() - 3
    taken = rest[:stages]
    ends, shadow, send_sem, recv_sem, end_send, end_recv, shadow_send, shadow_recv = rest[stages:]
    slices = through.shape[0]
    block_rows = blocks.shape[2]
    block_count = depth_count // 2
    stripes = 2 * light_count
    depth_at = lax.axis_index("depth")
    light_at = lax.axis_index("light")
    side = depth_at % 2
    pair = depth_at // 2
    stripe = light_at * 2 + side
    top = pair // (block_count // 2)
    low_bits = pair % (block_count // 2)

    def flipped(b):
        bit = (pair // (1 << b)) % 2
        return bit, (pair + (1 - 2 * bit) * (1 << b)) * 2 + side

    end_base = 2 * (side * (block_count // 2) + low_bits)
    source0 = 2 * low_bits + top
    source1 = 2 * (low_bits + block_count // 2) + top
    wanted = [(k != stripe, pair * 2 + k % 2, k // 2) for k in range(stripes)]
    wanted += [(depth_at >= 0, flipped(b)[1], light_at) for b in range(stages)]
    for x in range(2):
        wanted.append((end_base + x != depth_at, end_base + x, light_at))
    ends_from = [(source0 != depth_at, source0), (source1 != depth_at, source1)]
    wanted += [(exists, depth, light_at) for exists, depth in ends_from]
    greet(wanted)

    def shadow_copy(k, slot):
        return pltpu.make_async_remote_copy(
            src_ref=through,
            dst_ref=shadow.at[slot],
            send_sem=shadow_send.at[k],
            recv_sem=shadow_recv.at[slot],
            device_id=(pair * 2 + k % 2, k // 2),
            device_id_type=MESH,
        )

    for k in range(1, stripes):

        @pl.when(k > stripe)
        def _():
            shadow_copy(k, stripe).start()

    for z in range(slices):
        shadow[stripes, z] = jnp.ones((SUB, LANE), jnp.float32)
    for k in range(stripes - 1):

        @pl.when(k < stripe)
        def _():
            shadow_copy(k, k).wait_recv()
            for z in range(slices):
                shadow[stripes, z] = shadow[stripes, z] * shadow[k, z]

    lights = [shadow[stripes, z] for z in range(slices)]

    def finish(block):
        def one_row(i, carry):
            row = block * block_rows + i
            for c in range(3):
                value = plain[c, row]
                for z in range(slices):
                    value = value + lights[z] * lit[z * 3 + c, row]
                blocks[block, c, i] = value
            blocks[block, 3, i] = plain[3, row]
            return carry

        lax.fori_loop(0, block_rows, one_row, 0)

    def index_of(b, n, bit):
        uppers = block_count >> (b + 2)
        x, upper = n % 2, n // 2
        if uppers >= 2:
            later = (pair // (1 << (b + 1))) % 2
            rest = n % uppers
            x = rest % 2
            upper = 2 * (rest // 2) + (1 - later if n < uppers else later)
        return x + 2 * ((pair % (1 << b)) + (bit + 2 * upper) * (1 << b))

    def swap(b, n):
        bit, depth = flipped(b)
        slot = block_count - (block_count >> b) + n
        return pltpu.make_async_remote_copy(
            src_ref=blocks.at[index_of(b, n, 1 - bit)],
            dst_ref=taken[b].at[n],
            send_sem=send_sem.at[slot],
            recv_sem=recv_sem.at[slot],
            device_id=(depth, light_at),
            device_id_type=MESH,
        )

    count0 = block_count // 2
    bit0 = pair % 2
    for n in range(count0):
        finish(index_of(0, n, 1 - bit0))
        swap(0, n).start()
    for n in range(count0):
        finish(index_of(0, n, bit0))

    def blend_into(front_ref, back_ref, target_ref):
        for i in range(block_rows):
            clear = 1.0 - front_ref[3, i]
            for c in range(4):
                target_ref[c, i] = front_ref[c, i] + clear * back_ref[c, i]

    def blend(b, n):
        bit, depth = flipped(b)
        swap(b, n).wait_recv()
        mine = blocks.at[index_of(b, n, bit)]

        @pl.when(bit == 0)
        def _():
            blend_into(mine, taken[b].at[n], mine)

        @pl.when(bit == 1)
        def _():
            blend_into(taken[b].at[n], mine, mine)

    def end_copy(x, slot):
        return pltpu.make_async_remote_copy(
            src_ref=blocks.at[x + 2 * low_bits],
            dst_ref=ends.at[slot],
            send_sem=end_send.at[x],
            recv_sem=end_recv.at[slot],
            device_id=(end_base + x, light_at),
            device_id_type=MESH,
        )

    for b in range(stages):
        count = block_count >> (b + 1)
        bit, depth = flipped(b)
        if b + 1 < stages:
            for n in range(count // 2):
                blend(b, n)
            for n in range(count // 2):
                swap(b + 1, n).start()
            for n in range(count // 2, count):
                blend(b, n)
        else:
            for x in range(2):
                blend(b, x)

                @pl.when(end_base + x != depth_at)
                def _():
                    end_copy(x, top).start()

    stay = source0 == depth_at
    stay_late = source1 == depth_at
    mine = blocks.at[side + 2 * low_bits]

    @pl.when(jnp.logical_not(stay))
    def _():
        end_copy(0, 0).wait_recv()

    @pl.when(jnp.logical_not(stay_late))
    def _():
        end_copy(0, 1).wait_recv()

    @pl.when(stay)
    def _():
        blend_into(mine, ends.at[1], image)

    @pl.when(stay_late)
    def _():
        blend_into(ends.at[0], mine, image)

    @pl.when(jnp.logical_not(stay | stay_late))
    def _():
        blend_into(ends.at[0], ends.at[1], image)

    for b in range(stages):
        for n in range(block_count >> (b + 1)):
            swap(b, n).wait_send()
    for x in range(2):

        @pl.when(end_base + x != depth_at)
        def _():
            end_copy(x, top).wait_send()

    for k in range(1, stripes):

        @pl.when(k > stripe)
        def _():
            shadow_copy(k, stripe).wait_send()


def merge(plain, lit, through, depth_count, light_count):
    rows, slices = plain.shape[1], through.shape[0]
    f32 = jnp.float32
    block_count = depth_count // 2
    block = (4, rows // block_count, SUB, LANE)
    stages = depth_count.bit_length() - 3
    stripes = 2 * light_count
    dma = pltpu.SemaphoreType.DMA
    scratch = [pltpu.VMEM((block_count,) + block, f32)]
    scratch += [pltpu.VMEM((block_count >> (b + 1),) + block, f32) for b in range(stages)]
    scratch += [pltpu.VMEM((2,) + block, f32), pltpu.VMEM((stripes + 1, slices, SUB, LANE), f32)]
    scratch += [dma((block_count,)), dma((block_count,)), dma((2,)), dma((2,)), dma((stripes,)), dma((stripes,))]
    return pl.pallas_call(
        functools.partial(merge_kernel, depth_count, light_count),
        in_specs=[VMEM_SPEC] * 3,
        out_specs=VMEM_SPEC,
        out_shape=jax.ShapeDtypeStruct(block, f32),
        scratch_shapes=scratch,
        compiler_params=pltpu.CompilerParams(
            collective_id=1, has_side_effects=True, vmem_limit_bytes=40 * 1024 * 1024
        ),
    )(plain, lit, through)


def shards(density, labels, slice_order, extinction, albedo):
    depth_count = lax.axis_size("depth")
    light_count = lax.axis_size("light")
    slices, rows, columns = density.shape
    viewed, materials = reorder(density, labels, slice_order)
    heat, turned, stripe_labels = trade(viewed, materials, depth_count, light_count)
    plain, lit, through = shade(heat, turned, stripe_labels, extinction, albedo)
    return merge(plain, lit, through, depth_count, light_count).reshape(4, -1)


def solution(mesh):
    return jax.shard_map(
        shards,
        mesh=mesh,
        in_specs=(P("depth", "light", None), P("depth", "light", None), P("depth"), P(), P()),
        out_specs=P(None, ("light", "depth")),
        check_vma=False,
    )
```
